32 devices in a mesh: seq: 8 (over z, y), head: 4 (over x, core).
Axes of the slice: x: 2, y: 2, z: 4, core: 2. Of those that a mesh axis runs over, the one named last changes fastest.
Arguments:
- hidden_states: bfloat16 [4096, 4096], P('seq', 'head'), may hold values from -64 to 64
- out_grad: bfloat16 [4096, 4096], P('seq', 'head'), may hold values from -96 to 96
- encodings: bfloat16 [4096, 896], P('seq'), may hold values from -9 to 9
- w_query: bfloat16 [4096, 2048], P(None, 'head'), may hold values from -1 to 1
- w_key: bfloat16 [896, 2048], P(None, 'head'), may hold values from -1 to 1
- w_value: bfloat16 [896, 2048], P(None, 'head'), may hold values from -0.1875 to 0.1875
- w_out: bfloat16 [2048, 4096], P('head'), may hold values from -0.125 to 0.125
- neighbour_ids: int32 [64, 2], P('seq'), may hold values from 0 to 31, as said below
- neighbour_counts: int32 [64], P('seq'), may hold values from 1 to 2
Outputs:
- hidden_grad: bfloat16 [4096, 4096], P(('seq', 'head'))
- enc_grad: bfloat16 [4096, 896], P('seq', 'head')
The draws below stay inside these ranges and needn't reach their ends.
Inputs may be any that keep to these rules, and one draw needn't show every extreme that they name: `neighbour_ids`: record b lies in the shard of seq index b // 4. The 16 entries of the spans of one seq index name at most 2 records of any one shard, and exactly 2 of one shard that every seq index names so.
All inputs are finite; a program needn't handle non-finite values.
Results may differ from the reference program's by a relative error of at most 0.01.
The reference program's roundings to bfloat16 on the way (of `queries`, `attend_grad`, `soft_low`, `score_low` and `query_grad`) count: a program that leaves them out, or rounds other values in their place, can miss the bound.
Values may be sent and summed in bfloat16 or wider, within the bound.
No kernel may reach another device: no remote copies, remote signals or barrier semaphores. Data moves between devices by JAX's collectives and lax.ppermute only.
A program may use at most 128 MiB of HBM per device.

```python
import math
import jax
import jax.numpy as jnp
from jax import lax

D = 4096
HEADS = 16
HD = 128
ENC = 896
SPAN = 64
NEIGH = 2
RET = 128
SP_DEV = 8
REC_DEV = 4
HC = 2048
TOKENS = 4096
SPANS = 64
RECORDS = 32
CAP = 2
N_SEQ = 8
N_HEAD = 4


def neighbour_table(base_key):
    inner_key = jax.random.fold_in(base_key, 101)
    owners = RECORDS // REC_DEV
    devices = SPANS // SP_DEV
    ask_total = SP_DEV * NEIGH
    hot_key, level_key, device_keys = jax.random.split(inner_key, 3)
    hot_owner = jax.random.randint(hot_key, (), 0, owners)
    hot_level = jax.random.randint(level_key, (owners,), 0, 2)
    hot_level = jnp.where(jnp.arange(owners) == hot_owner, 2, hot_level)
    pair_low = max(1, -(-(ask_total - owners) // (CAP - 1)))
    pair_high = ask_total // CAP

    def one_device(device_key):
        score_key, pair_key, start_key, order_key = jax.random.split(device_key, 4)
        noise_draw = jax.random.randint(score_key, (owners,), 0, 65536)
        scores = (hot_level * 65536 + noise_draw) * 64 + jnp.arange(owners)
        ranked = lax.top_k(scores, owners)[1]
        pair_count = jax.random.randint(pair_key, (), pair_low, pair_high + 1)
        slot_index = jnp.arange(ask_total)
        paired = slot_index < CAP * pair_count
        owner_rank = jnp.where(paired, slot_index // CAP, pair_count + slot_index - CAP * pair_count)
        within = jnp.where(paired, slot_index % CAP, 0)
        owner_of = ranked[owner_rank]
        start_record = jax.random.randint(start_key, (owners,), 0, REC_DEV)
        local_record = (start_record[owner_of] + within) % REC_DEV
        record_ids = owner_of * REC_DEV + local_record
        return record_ids[jax.random.permutation(order_key, ask_total)]
    record_table = jax.vmap(one_device)(jax.random.split(device_keys, devices))
    return record_table.reshape(SPANS, NEIGH).astype(jnp.int32)


def key_matrix(base_key):
    inner_key = jax.random.fold_in(base_key, 404)
    return jnp.clip(jax.random.normal(inner_key, (ENC, HC), jnp.float32), -6.0, 6.0) / math.sqrt(ENC)


def draw_neighbour_ids(key, part):
    return neighbour_table(key)


def draw_encodings(key, part):
    inner_key = jax.random.fold_in(key, 203)
    return jnp.clip(jax.random.normal(inner_key, (RECORDS * RET, ENC), jnp.float32), -6.0, 6.0).astype(jnp.bfloat16)


def draw_w_key(key, part):
    matrix = key_matrix(key)
    return matrix.astype(jnp.bfloat16)


def draw_w_query(key, part):
    inner_key = jax.random.fold_in(key, 505)
    matrix = jnp.clip(jax.random.normal(inner_key, (D, HC), jnp.float32), -6.0, 6.0) / math.sqrt(D)
    return matrix.astype(jnp.bfloat16)


def draw_hidden_states(key, part):
    inner_key = jax.random.fold_in(key, 303)
    value_key = jax.random.fold_in(inner_key, 0)
    return jnp.clip(jax.random.normal(value_key, (TOKENS, D), jnp.float32), -6.0, 6.0).astype(jnp.bfloat16)


def with_ends(result, rng, smallest, high):
    longest = result.shape.index(max(result.shape))
    spots = []
    for shift in (0, 1):
        where = [jax.random.randint(jax.random.fold_in(rng, axis), (), 0, length) for axis, length in enumerate(result.shape)]
        where[longest] = (where[longest] + shift) % result.shape[longest]
        spots.append(tuple(where))
    return result.at[spots[0]].set(smallest).at[spots[1]].set(high)


def steps_of(key, dims, cuts, smallest, high):
    def one(position, shards_of):
        draws = jax.random.uniform(jax.random.fold_in(jax.random.fold_in(key, 6), position), (shards_of,), jnp.float32, smallest / len(cuts), high / len(cuts))
        return jnp.repeat(jnp.exp(draws), dims[position] // shards_of).reshape((-1,) + (1,) * (len(dims) - position - 1))

    factor_of = one(*cuts[0])
    for cut in cuts[1:]:
        factor_of = factor_of * one(*cut)
    return factor_of


def gaussian(rng, shape, scale, bound, pieces=(), held_as=jnp.bfloat16):
    drawn = jax.random.normal(rng, shape, jnp.float32) * scale
    if len(pieces) > 0:
        drawn = steps_of(rng, shape, pieces, -0.22, 0.18) * drawn
    return jnp.clip(drawn, min=-bound, max=bound).astype(held_as)


def setup_inputs(seed: int = 0) -> dict:
    keys = jax.random.split(jax.random.key(seed), 10)
    return {
        "hidden_states": draw_hidden_states(jax.random.fold_in(keys[9], 71), 0),
        "out_grad": gaussian(keys[1], (TOKENS, D), 16.0, 96.0, ((0, 8), (1, 4))),
        "encodings": draw_encodings(jax.random.fold_in(keys[9], 71), 0),
        "w_query": draw_w_query(jax.random.fold_in(keys[9], 71), 0),
        "w_key": draw_w_key(jax.random.fold_in(keys[9], 71), 0),
        "w_value": gaussian(keys[5], (ENC, HC), ENC ** -0.5, 0.1875, ((1, 4),)),
        "w_out": gaussian(keys[6], (HC, D), HC ** -0.5, 0.125, ((0, 4),)),
        "neighbour_ids": draw_neighbour_ids(jax.random.fold_in(keys[9], 71), 0),
        "neighbour_counts": with_ends(jax.random.randint(keys[8], (SPANS,), 1, NEIGH + 1), jax.random.fold_in(keys[8], 1), 1, NEIGH).astype(jnp.int32),
    }


def to_float(value):
    return lax.optimization_barrier(value).astype(jnp.float32)

def span_attention(queries, attend_grad, key_rows, value_rows, record_counts, heads_here):
    row_count = queries.shape[0]
    spans_here = row_count // SPAN
    shift_by = SPAN - 1
    score_scale = 1.0 / math.sqrt(HD)
    highest = lax.Precision.HIGHEST
    has_keys = jnp.arange(row_count) < row_count - shift_by
    query_rows = to_float(jnp.roll(queries, -shift_by, axis=0)).reshape(spans_here, SPAN, heads_here, HD)
    grad_rows = jnp.where(has_keys[:, None], jnp.roll(attend_grad, -shift_by, axis=0), jnp.zeros((), jnp.bfloat16))
    grad_rows = to_float(grad_rows).reshape(spans_here, SPAN, heads_here, HD)
    key_spans = to_float(key_rows).reshape(spans_here, NEIGH * RET, heads_here, HD)
    value_spans = to_float(value_rows).reshape(spans_here, NEIGH * RET, heads_here, HD)
    in_use = jnp.arange(NEIGH)[None, :] < record_counts[:, None]
    key_in_use = jnp.repeat(in_use, RET, axis=1)
    scores = jnp.einsum('cqhd,ckhd->chqk', query_rows, key_spans, precision=highest) * score_scale
    scores = jnp.where(key_in_use[:, None, None, :], scores, -jnp.inf)
    row_top = lax.optimization_barrier(jnp.max(scores, axis=-1, keepdims=True))
    exponent = jnp.exp(scores - row_top)
    soft_weights = exponent / lax.optimization_barrier(jnp.sum(exponent, axis=-1, keepdims=True))
    soft_low = to_float(soft_weights.astype(jnp.bfloat16))
    outputs = jnp.einsum('chqk,ckhd->cqhd', soft_low, value_spans, precision=highest)
    row_delta = lax.optimization_barrier(jnp.sum(grad_rows * outputs, axis=-1))
    prob_grad = jnp.einsum('cqhd,ckhd->chqk', grad_rows, value_spans, precision=highest)
    score_grad = soft_weights * (prob_grad - jnp.transpose(row_delta, (0, 2, 1))[..., None])
    score_low = to_float(score_grad.astype(jnp.bfloat16))
    query_grad = (jnp.einsum('chqk,ckhd->cqhd', score_low, key_spans, precision=highest) * score_scale).astype(jnp.bfloat16)
    key_grad = (jnp.einsum('chqk,cqhd->ckhd', score_low, query_rows, precision=highest) * score_scale).astype(jnp.bfloat16)
    value_grad = jnp.einsum('chqk,cqhd->ckhd', soft_low, grad_rows, precision=highest).astype(jnp.bfloat16)
    columns = heads_here * HD
    query_grad = jnp.roll(query_grad.reshape(row_count, columns), shift_by, axis=0)
    pair_total = spans_here * NEIGH
    return (query_grad, key_grad.reshape(pair_total, RET, columns), value_grad.reshape(pair_total, RET, columns))

def reference(hidden_states, out_grad, encodings, w_query, w_key, w_value, w_out, neighbour_ids, neighbour_counts):
    window = SP_DEV * SPAN
    all_columns = HEADS * HD
    group_width = all_columns // N_HEAD
    contract_last = (((1,), (1,)), ((), ()))
    highest = lax.Precision.HIGHEST
    keys_all = jnp.dot(encodings, w_key, preferred_element_type=jnp.float32).astype(jnp.bfloat16).reshape(RECORDS, RET, all_columns)
    values_all = jnp.dot(encodings, w_value, preferred_element_type=jnp.float32).astype(jnp.bfloat16).reshape(RECORDS, RET, all_columns)

    def one_window(running, inputs):
        key_acc, value_acc = running
        hidden_win, grad_win, record_ids, record_counts = inputs
        flat_ids = record_ids.reshape(SP_DEV * NEIGH)
        queries = jnp.dot(hidden_win, w_query, preferred_element_type=jnp.float32).astype(jnp.bfloat16)
        attend_grad = lax.dot_general(grad_win, w_out, contract_last, preferred_element_type=jnp.float32).astype(jnp.bfloat16)
        query_grad, key_grad, value_grad = span_attention(queries, attend_grad, keys_all[flat_ids], values_all[flat_ids], record_counts, HEADS)
        summed = jnp.zeros((window, D), jnp.float32)
        for group_at in range(N_HEAD):
            lower = group_at * group_width
            partial_value = lax.dot_general(query_grad[:, lower:lower + group_width], w_query[:, lower:lower + group_width], contract_last, preferred_element_type=jnp.float32)
            summed = summed + to_float(partial_value.astype(jnp.bfloat16))
        key_acc = key_acc.at[flat_ids].add(to_float(key_grad))
        value_acc = value_acc.at[flat_ids].add(to_float(value_grad))
        return ((key_acc, value_acc), summed.astype(jnp.bfloat16))
    zero_acc = jnp.zeros((RECORDS, RET, all_columns), jnp.float32)
    inputs = (hidden_states.reshape(N_SEQ, window, D), out_grad.reshape(N_SEQ, window, D), neighbour_ids.reshape(N_SEQ, SP_DEV, NEIGH), neighbour_counts.reshape(N_SEQ, SP_DEV))
    (key_acc, value_acc), windows = lax.scan(one_window, (zero_acc, zero_acc), inputs)
    enc_grad = lax.dot_general(key_acc.reshape(RECORDS * RET, all_columns), w_key.astype(jnp.float32), contract_last, precision=highest)
    enc_grad = enc_grad + lax.dot_general(value_acc.reshape(RECORDS * RET, all_columns), w_value.astype(jnp.float32), contract_last, precision=highest)
    return (windows.reshape(TOKENS, D), enc_grad.astype(jnp.bfloat16))
```

```python
import functools
import math

import jax
import jax.numpy as jnp
from jax import lax
from jax.experimental import pallas as pl
from jax.experimental.pallas import tpu as pltpu
from jax.sharding import PartitionSpec as P


HD = 128
SPAN = 64
NEIGH = 2
RET = 128
CORES = 2
CAP = 2
HALF = RET // CORES


BF16 = jnp.bfloat16
F32 = jnp.float32
F16 = jnp.float16
NT = (((1,), (1,)), ((), ()))
TN = (((0,), (0,)), ((), ()))
VM = pltpu.MemorySpace.VMEM
SM = pltpu.MemorySpace.SMEM


def swap(value, axis, distance):
    count = lax.axis_size(axis)
    return lax.ppermute(value, axis, [(i, i ^ distance) for i in range(count)])


def after(value, *others):
    return lax.optimization_barrier((value,) + others)[0]


def table_by_distance(row, count):
    table = row
    distance = 1
    while distance < count:
        table = jnp.concatenate([table, swap(table, "seq", distance)], axis=0)
        distance *= 2
    return table


def pack(value, bound):
    return (value * (32768.0 / bound)).astype(F16)


def unpack(value, bound):
    return value.astype(F32) * (bound / 32768.0)


def slots_of(named, per_shard):
    slots = [jnp.int32(0)] * CAP
    seen = jnp.int32(0)
    for record in range(per_shard):
        bit = (named >> record) & 1
        for slot in range(CAP):
            slots[slot] = jnp.where((bit == 1) & (seen == slot), record, slots[slot])
        seen = seen + bit
    return slots


def request_kernel(place_ref, ids_ref, enc_ref, asked_ref, *blocks, seq_count, per_shard):
    me = place_ref[0]
    core = place_ref[1] % CORES
    entries = ids_ref.shape[0] * ids_ref.shape[1] // seq_count
    width = ids_ref.shape[1]
    for distance in reversed(range(seq_count)):
        named = jnp.int32(0)
        for entry in range(entries):
            at = distance * entries + entry
            record = ids_ref[at // width, at % width]
            hit = record // per_shard == me
            named = named | jnp.where(hit, 1 << (record % per_shard), 0)
        slots = slots_of(named, per_shard)
        for slot in range(CAP):
            start = pl.multiple_of(slots[slot] * RET + core * HALF, HALF)
            blocks[distance][slot] = enc_ref[pl.ds(start, HALF), :]
            if distance == 0:
                other = pl.multiple_of(slots[slot] * RET + (1 - core) * HALF, HALF)
                blocks[seq_count][slot] = enc_ref[pl.ds(other, HALF), :]
        chosen = slots[0]
        for slot in range(1, CAP):
            chosen = jnp.where(core == slot, slots[slot], chosen)
        asked_ref[distance] = chosen


def request(place, ids_table, encodings, seq_count):
    per_shard = encodings.shape[0] // RET
    block = jax.ShapeDtypeStruct((CAP, HALF, encodings.shape[1]), BF16)
    return pl.pallas_call(
        functools.partial(request_kernel, seq_count=seq_count, per_shard=per_shard),
        out_shape=[jax.ShapeDtypeStruct((seq_count,), jnp.int32)] + [block] * (seq_count + 1),
        in_specs=[pl.BlockSpec(memory_space=SM)] * 2 + [pl.BlockSpec(memory_space=VM)],
        out_specs=[pl.BlockSpec(memory_space=SM)]
        + [pl.BlockSpec(memory_space=VM)] * (seq_count + 1),
        cost_estimate=pl.CostEstimate(
            flops=0, transcendentals=0, bytes_accessed=4 * encodings.size * 2
        ),
        name="request",
    )(place, ids_table, encodings)


def plan_kernel(place_ref, ids_ref, plan_ref, *, per_shard):
    me = place_ref[0]
    rows, cols = ids_ref.shape
    entries = rows * cols
    records = [ids_ref[entry // cols, entry % cols] for entry in range(entries)]
    for entry in range(entries):
        owner = records[entry] // per_shard
        local = records[entry] % per_shard
        below = jnp.int32(0)
        earlier = jnp.int32(0)
        for other in range(entries):
            same = records[other] // per_shard == owner
            below = below | jnp.where(same, 1 << (records[other] % per_shard), 0)
            if other < entry:
                earlier = earlier | jnp.where(records[other] == records[entry], 1, 0)
        below = below & ((1 << local) - 1)
        rank = jnp.int32(0)
        for bit_at in range(per_shard):
            rank = rank + ((below >> bit_at) & 1)
        plan_ref[entry] = owner ^ me
        plan_ref[entries + entry] = rank
        plan_ref[2 * entries + entry] = earlier


def plan_entries(place, ids, per_shard):
    return pl.pallas_call(
        functools.partial(plan_kernel, per_shard=per_shard),
        out_shape=jax.ShapeDtypeStruct((3 * ids.size,), jnp.int32),
        in_specs=[pl.BlockSpec(memory_space=SM)] * 2,
        out_specs=pl.BlockSpec(memory_space=SM),
        cost_estimate=pl.CostEstimate(flops=0, transcendentals=0, bytes_accessed=1 << 20),
        name="plan",
    )(place, ids)


def project_kernel(place_ref, *refs, count):
    pieces = refs[: 2 * count]
    wk_ref, wv_ref = refs[2 * count : 2 * count + 2]
    key_ref, value_ref, rows = refs[-3:]
    core = place_ref[1] % CORES

    @pl.when(pl.program_id(0) == 0)
    def _():
        for block in range(count):
            for source, half in ((pieces[2 * block], core), (pieces[2 * block + 1], 1 - core)):
                for slot in range(CAP):
                    at = pl.multiple_of((block * CAP + slot) * RET + half * HALF, HALF)
                    rows[pl.ds(at, HALF), :] = source[slot]

    for weight, target in ((wk_ref, key_ref), (wv_ref, value_ref)):
        target[...] = jnp.dot(rows[...], weight[...], preferred_element_type=F32).astype(BF16)


def project(place, pieces, w_key, w_value, held, group, groups):
    depth, columns = w_key.shape
    count = len(pieces) // 2
    height = count * CAP * RET
    wide = min(columns, 256)
    shape = jax.ShapeDtypeStruct((groups * height, columns), BF16)
    whole = lambda a: pl.BlockSpec(a.shape, lambda i: (0,) * a.ndim)
    weight_spec = pl.BlockSpec((depth, wide), lambda i: (0, i))
    out_spec = pl.BlockSpec((height, wide), lambda i: (group, i))
    extra = list(held) if held is not None else []
    args = len(pieces) + 2
    return pl.pallas_call(
        functools.partial(project_kernel, count=count),
        grid=(columns // wide,),
        out_shape=[shape, shape],
        in_specs=[pl.BlockSpec(memory_space=SM)]
        + [whole(a) for a in pieces]
        + [weight_spec] * 2
        + [pl.BlockSpec(memory_space=pl.ANY)] * len(extra),
        out_specs=[out_spec, out_spec],
        scratch_shapes=[pltpu.VMEM((height, depth), BF16)],
        input_output_aliases={args + 1: 0, args + 2: 1} if extra else {},
        cost_estimate=pl.CostEstimate(
            flops=4 * height * w_key.size,
            transcendentals=0,
            bytes_accessed=4 * (w_key.size + height * columns),
        ),
        name="project",
    )(place, *pieces, w_key, w_value, *extra)


def attend_kernel(
    place_ref,
    plan_ref,
    counts_ref,
    tops_ref,
    q_ref,
    g_ref,
    k_ref,
    v_ref,
    ready_query,
    ready_pair,
    qg_mine,
    qg_theirs,
    bound_ref,
    mine_far,
    mine_near,
    theirs_far,
    theirs_near,
    q_rows,
    g_rows,
    qg_rows,
    kv_pair,
    kv_all,
    highest,
    sems,
):
    core = place_ref[1] % CORES
    rows, columns = q_ref.shape
    heads = columns // HD
    shift = SPAN - 1
    spans = rows // SPAN
    entries = spans * NEIGH
    seq_count = kv_all.shape[0] // (CAP * RET)
    full = rows - SPAN
    scale = 1.0 / math.sqrt(HD)
    for source, target in ((q_ref, q_rows), (g_ref, g_rows)):
        target[0:full, :] = source[shift : shift + full, :].astype(BF16)
        first = lax.broadcasted_iota(jnp.int32, (SPAN, columns), 0) == 0
        last = jnp.broadcast_to(source[rows - 1 : rows, :], (SPAN, columns))
        target[full:rows, :] = jnp.where(first, last, 0.0).astype(BF16)
    kv_all[...] = jnp.zeros_like(kv_all)
    highest[...] = jnp.zeros_like(highest)

    def fold(value):
        return jnp.max(jnp.abs(value).reshape(-1, 8, HD), axis=0)

    def one_span(span, carry):
        base = pl.multiple_of(span * SPAN, SPAN)
        two = counts_ref[span] > 1
        dist = [plan_ref[span * NEIGH + n] for n in range(NEIGH)]
        rank = [plan_ref[entries + span * NEIGH + n] for n in range(NEIGH)]
        again = [plan_ref[2 * entries + span * NEIGH + n] for n in range(NEIGH)]
        key_at = [pl.multiple_of((dist[n] * CAP + rank[n]) * RET, RET) for n in range(NEIGH)]
        column_at = lax.broadcasted_iota(jnp.int32, (SPAN, NEIGH * RET), 1)
        in_use = (column_at < RET) | two
        each = range(heads)
        lanes = [slice(head * HD, (head + 1) * HD) for head in each]
        q = [q_rows[pl.ds(base, SPAN), lanes[h]] for h in each]
        g = [g_rows[pl.ds(base, SPAN), lanes[h]] for h in each]
        k = [
            jnp.concatenate([k_ref[pl.ds(at, RET), lanes[h]] for at in key_at], axis=0)
            for h in each
        ]
        v = [
            jnp.concatenate([v_ref[pl.ds(at, RET), lanes[h]] for at in key_at], axis=0)
            for h in each
        ]
        scores = [
            lax.dot_general(q[h], k[h], NT, preferred_element_type=F32) * scale for h in each
        ]
        prob = [lax.dot_general(g[h], v[h], NT, preferred_element_type=F32) for h in each]
        scores = [jnp.where(in_use, scores[h], -jnp.inf) for h in each]
        top = [jnp.max(scores[h], axis=-1, keepdims=True) for h in each]
        exponent = [jnp.exp(scores[h] - top[h]) for h in each]
        soft = [exponent[h] / jnp.sum(exponent[h], axis=-1, keepdims=True) for h in each]
        low = [soft[h].astype(BF16) for h in each]
        out = [jnp.dot(low[h], v[h], preferred_element_type=F32) for h in each]
        vg = [lax.dot_general(low[h], g[h], TN, preferred_element_type=F32) for h in each]
        delta = [jnp.sum(g[h].astype(F32) * out[h], axis=-1, keepdims=True) for h in each]
        score_low = [(soft[h] * (prob[h] - delta[h])).astype(BF16) for h in each]
        qg = [jnp.dot(score_low[h], k[h], preferred_element_type=F32) * scale for h in each]
        kg = [
            lax.dot_general(score_low[h], q[h], TN, preferred_element_type=F32) * scale
            for h in each
        ]
        for h in each:
            qg_rows[pl.ds(base, SPAN), lanes[h]] = qg[h]
            kv_pair[:, lanes[h]] = kg[h].astype(BF16)
            kv_pair[:, columns + h * HD : columns + (h + 1) * HD] = vg[h].astype(BF16)
        for at, made in enumerate((qg, kg, vg)):
            most = highest[at]
            for h in each:
                most = jnp.maximum(most, fold(made[h]))
            highest[at] = most
        for n in range(NEIGH):
            made = slice(n * RET, (n + 1) * RET)
            which = jnp.where(rank[n] == core, 0, 1)
            at = pl.multiple_of((which * seq_count + dist[n]) * RET, RET)

            @pl.when(again[n] == 0)
            def _():
                kv_all[pl.ds(at, RET), :] = kv_pair[made, :]

            @pl.when(again[n] != 0)
            def _():
                total = kv_all[pl.ds(at, RET), :].astype(F32) + kv_pair[made, :].astype(F32)
                kv_all[pl.ds(at, RET), :] = total.astype(BF16)

        return carry

    lax.fori_loop(0, spans, one_span, 0)
    half = seq_count // 2 * RET
    copies = []
    for at, target in enumerate((mine_near, mine_far, theirs_near, theirs_far)):
        copies.append(
            pltpu.make_async_copy(kv_all.at[pl.ds(at * half, half), :], target, sems.at[at])
        )
    for copy in copies:
        copy.start()
    moved = jnp.concatenate(
        [jnp.zeros((shift, columns), F32), qg_rows[0 : rows - shift, :]], axis=0
    )
    qg_rows[...] = moved
    pieces, take = qg_mine.shape[:2]
    for piece in range(pieces):
        for target, which in ((qg_mine, core), (qg_theirs, 1 - core)):
            at = pl.multiple_of((piece * CORES + which) * take, take)
            target[piece] = qg_rows[pl.ds(at, take), :].astype(BF16)
    most = [jnp.max(highest[at]) for at in range(3)]
    hidden_bound = most[0] * tops_ref[0] * columns
    enc_bound = (most[1] * tops_ref[1] + most[2] * tops_ref[2]) * (columns * entries)
    upper = lax.broadcasted_iota(jnp.int32, bound_ref.shape, 0) < 4
    bound_ref[...] = jnp.where(upper, hidden_bound, enc_bound) * 1.03125 + 1e-30
    for copy in copies:
        copy.wait()


def attend(place, plan, counts, tops, q, g, key_rows, value_rows, ready, chips):
    rows, columns = q.shape
    height = key_rows.shape[0]
    take = rows // (chips * CORES)
    qg = jax.ShapeDtypeStruct((chips, take, columns), BF16)
    kv = jax.ShapeDtypeStruct((height // 4, 2 * columns), BF16)
    bound = jax.ShapeDtypeStruct((8, HD), F32)
    flops = 6 * 2 * rows * NEIGH * RET * columns
    anywhere = pl.BlockSpec(memory_space=pl.ANY)
    return pl.pallas_call(
        attend_kernel,
        out_shape=[qg, qg, bound, kv, kv, kv, kv],
        in_specs=[pl.BlockSpec(memory_space=SM)] * 4
        + [pl.BlockSpec(memory_space=VM)] * 4
        + [anywhere] * 2,
        out_specs=[pl.BlockSpec(memory_space=VM)] * 3 + [anywhere] * 4,
        scratch_shapes=[
            pltpu.VMEM((rows, columns), BF16),
            pltpu.VMEM((rows, columns), BF16),
            pltpu.VMEM((rows, columns), F32),
            pltpu.VMEM((NEIGH * RET, 2 * columns), BF16),
            pltpu.VMEM((height, 2 * columns), BF16),
            pltpu.VMEM((3, 8, HD), F32),
            pltpu.SemaphoreType.DMA((4,)),
        ],
        compiler_params=pltpu.CompilerParams(vmem_limit_bytes=40 << 20),
        cost_estimate=pl.CostEstimate(
            flops=8 * flops,
            transcendentals=rows * NEIGH * RET * columns // HD,
            bytes_accessed=8 * q.size + 8 * key_rows.size,
        ),
        name="attend",
    )(place, plan, counts, tops, q, g, key_rows, value_rows, *ready)


def collect_kernel(asked_ref, place_ref, *refs):
    blocks = refs[:-3]
    mine_ref, theirs_ref, total = refs[-3:]
    core = place_ref[1] % CORES
    total[...] = jnp.zeros_like(total)
    for distance, block in enumerate(blocks):
        at = pl.multiple_of(asked_ref[distance] * RET, RET)
        total[:, pl.ds(at, RET)] += block[...].astype(F32)
    take = mine_ref.shape[0]
    for target, which in ((mine_ref, core), (theirs_ref, 1 - core)):
        target[...] = total[pl.ds(pl.multiple_of(which * take, take), take), :]


def collect(asked, place, blocks, per_shard):
    height = blocks[0].shape[0]
    half = jax.ShapeDtypeStruct((height // CORES, per_shard * RET), F32)
    return pl.pallas_call(
        collect_kernel,
        out_shape=[half, half],
        in_specs=[pl.BlockSpec(memory_space=SM)] * 2
        + [pl.BlockSpec(memory_space=VM)] * len(blocks),
        out_specs=[pl.BlockSpec(memory_space=VM)] * 2,
        scratch_shapes=[pltpu.VMEM((height, per_shard * RET), F32)],
        cost_estimate=pl.CostEstimate(
            flops=2 * len(blocks) * blocks[0].size,
            transcendentals=0,
            bytes_accessed=4 * len(blocks) * blocks[0].size,
        ),
        name="collect",
    )(asked, place, *blocks)


def shards(
    hidden_states,
    out_grad,
    encodings,
    w_query,
    w_key,
    w_value,
    w_out,
    neighbour_ids,
    neighbour_counts,
):
    seq_count = lax.axis_size("seq")
    head_count = lax.axis_size("head")
    chips = head_count // CORES
    seq_at = lax.axis_index("seq")
    head_at = lax.axis_index("head")
    chip_at = head_at // CORES
    place = jnp.stack([seq_at, head_at]).astype(jnp.int32)
    per_shard = encodings.shape[0] // RET
    features = hidden_states.shape[1]
    width = encodings.shape[1]

    far = [(hidden_states, out_grad)]
    for step in range(1, chips):
        far.append(
            (
                swap(hidden_states, "head", step * CORES),
                swap(out_grad, "head", step * CORES),
            )
        )
    ids_table = table_by_distance(neighbour_ids.reshape(1, -1), seq_count)
    asked, *blocks = request(place, ids_table, encodings, seq_count)
    own_half = blocks.pop()
    mine = [None] * seq_count
    for distance in reversed(range(1, seq_count)):
        mine[distance] = swap(blocks[distance], "seq", distance)
    pieces = [(blocks[0], own_half)]
    for distance in range(1, seq_count):
        pieces.append((mine[distance], swap(mine[distance], "head", 1)))
    plan = plan_entries(after(place, asked), neighbour_ids, per_shard)

    w_query_near = swap(w_query, "head", 1)
    w_pair = jnp.concatenate([after(w_key, asked), w_value], axis=1)
    w_pair_near = swap(w_pair, "head", 1)
    late = after((w_query, w_key, w_value), asked)
    tops = jnp.stack([jnp.max(jnp.abs(w)).astype(F32) for w in late])

    held = None
    groups = 2
    per_group = seq_count // groups
    for group in range(groups):
        chosen = pieces[group * per_group : (group + 1) * per_group]
        flat = [piece for pair in chosen for piece in pair]
        held = project(place, flat, w_key, w_value, held, group, groups)
    key_rows, value_rows = held

    query_sum = jnp.zeros((), F32)
    grad_sum = jnp.zeros((), F32)
    for step in range(chips):
        for side in range(CORES):
            hidden_piece, grad_piece = far[step]
            if side:
                hidden_piece = swap(hidden_piece, "head", 1)
                grad_piece = swap(grad_piece, "head", 1)
            elif step == 0:
                hidden_piece, grad_piece = after((hidden_piece, grad_piece), asked)
            block_at = (head_at ^ (step * CORES + side)) * features
            query_sum = query_sum + jnp.dot(
                hidden_piece,
                lax.dynamic_slice_in_dim(w_query, block_at, features, 0),
                preferred_element_type=F32,
            )
            grad_sum = grad_sum + lax.dot_general(
                grad_piece,
                lax.dynamic_slice_in_dim(w_out, block_at, features, 1),
                NT,
                preferred_element_type=F32,
            )

    qg_mine, qg_theirs, bound, mine_far, mine_near, theirs_far, theirs_near = attend(
        place,
        plan,
        neighbour_counts,
        tops,
        query_sum,
        grad_sum,
        key_rows,
        value_rows,
        (w_query_near, w_pair_near),
        chips,
    )
    far_near = swap(theirs_far, "head", 1)
    total_bound = bound
    for d in range(1, head_count):
        total_bound = total_bound + swap(bound, "head", d)
    qg_near = swap(qg_theirs, "head", 1)
    near_near = swap(theirs_near, "head", 1)
    hidden_bound = total_bound[0, 0]
    enc_bound = total_bound[4, 0]

    strip = width // chips

    def enc_strip(step, kv, near_kv, *earlier):
        at = (chip_at ^ step) * strip
        own = lax.dynamic_slice_in_dim(w_pair, at, strip, 0)
        near = lax.dynamic_slice_in_dim(w_pair_near, at, strip, 0)
        if earlier:
            kv = after(kv, *earlier)
        return lax.dot_general(own, kv, NT, preferred_element_type=F32) + lax.dot_general(
            near, near_kv, NT, preferred_element_type=F32
        )

    halves = ((mine_far, far_near, seq_count // 2), (mine_near, near_near, 0))
    packed = []
    sent = []
    for kv, near_kv, first in halves:
        made = [
            pack(enc_strip(step, kv, near_kv, *packed), enc_bound) for step in range(1, chips)
        ]
        packed = packed + made
        sent.append([swap(made[step - 1], "head", step * CORES) for step in range(1, chips)])
    take = qg_mine.shape[1]
    rows_of = lambda v: v.reshape(chips * take, v.shape[2])
    own_part = lax.dot_general(
        after(rows_of(qg_mine), *packed), w_query, NT, preferred_element_type=F32
    )
    near_part = lax.dot_general(
        rows_of(qg_near), w_query_near, NT, preferred_element_type=F32
    )
    own_part, near_part = lax.optimization_barrier(
        (own_part.astype(BF16), near_part.astype(BF16))
    )

    def hidden_rows(step):
        at = (chip_at ^ step) * take
        return lax.dynamic_slice_in_dim(own_part, at, take, 0).astype(
            F32
        ) + lax.dynamic_slice_in_dim(near_part, at, take, 0).astype(F32)

    hidden_packed = [pack(hidden_rows(step), hidden_bound) for step in range(1, chips)]
    hidden_sent = [swap(hidden_packed[step - 1], "head", step * CORES) for step in range(1, chips)]
    total_table = table_by_distance(after(total_bound, *packed)[4:5, :], seq_count)

    back = [None] * seq_count
    done = hidden_packed
    for (kv, near_kv, first), arrived in zip(halves, sent):
        enc_sum = lax.optimization_barrier(enc_strip(0, kv, near_kv, *done))
        for piece in arrived:
            enc_sum = enc_sum + unpack(piece, enc_bound)
        made = []
        for distance in range(first, first + seq_count // 2):
            at = (distance - first) * RET
            piece = enc_sum[:, at : at + RET]
            if distance > 0:
                made.append(pack(piece, enc_bound))
                piece = swap(made[-1], "seq", distance)
                piece = unpack(piece, total_table[distance, 0])
            back[distance] = piece
        done = made
    enc_mine, enc_theirs = collect(asked, place, back, per_shard)
    enc_grad = (enc_mine + swap(enc_theirs, "head", 1)).T.astype(BF16)

    hidden_sum = hidden_rows(0)
    for piece in hidden_sent:
        hidden_sum = hidden_sum + unpack(piece, hidden_bound)
    return (hidden_sum.astype(BF16), enc_grad)


def solution(mesh):
    return jax.shard_map(
        shards,
        mesh=mesh,
        in_specs=(
            P("seq", "head"),
            P("seq", "head"),
            P("seq", None),
            P(None, "head"),
            P(None, "head"),
            P(None, "head"),
            P("head", None),
            P("seq", None),
            P("seq"),
        ),
        out_specs=(P(("seq", "head"), None), P("seq", "head")),
        check_vma=False,
    )
```

```python
import functools
import math

import jax
import jax.numpy as jnp
from jax import lax
from jax.experimental import pallas as pl
from jax.experimental.pallas import tpu as pltpu
from jax.sharding import PartitionSpec as P


HD = 128
SPAN = 64
NEIGH = 2
RET = 128
CORES = 2
CAP = 2
HALF = RET // CORES


BF16 = jnp.bfloat16
F32 = jnp.float32
I16 = jnp.int16
TILE = 16
NT = (((1,), (1,)), ((), ()))
TN = (((0,), (0,)), ((), ()))
VM = pltpu.MemorySpace.VMEM
SM = pltpu.MemorySpace.SMEM


def room(*arrays, spare=2 << 20):
    total = sum(math.prod(a.shape) * jnp.dtype(a.dtype).itemsize for a in arrays)
    return pltpu.CompilerParams(vmem_limit_bytes=int(total) + spare)


def swap(value, axis, distance):
    count = lax.axis_size(axis)
    return lax.ppermute(value, axis, [(i, i ^ distance) for i in range(count)])


def after(value, *others):
    return lax.optimization_barrier((value,) + others)[0]


def table_by_distance(row, count):
    table = row
    distance = 1
    while distance < count:
        table = jnp.concatenate([table, swap(table, "seq", distance)], axis=0)
        distance *= 2
    return table


def encode(value, axis):
    most = jnp.max(jnp.abs(value), axis=axis, keepdims=True)
    power = jnp.ceil(jnp.log2(jnp.maximum(most, 1e-30)))
    scaled = value * jnp.exp2(14.0 - power)
    code = (scaled + jnp.where(scaled >= 0, 0.5, -0.5)).astype(jnp.int32)
    return code.astype(I16), power.astype(jnp.int32)


def decode(code, power):
    unit = jnp.exp2(power.astype(jnp.int32).astype(F32) - 14.0)
    return code.astype(jnp.int32).astype(F32) * unit


def split_record(record, per_shard):
    if per_shard & (per_shard - 1) == 0:
        return record >> (per_shard.bit_length() - 1), record & (per_shard - 1)
    return lax.div(record, per_shard), lax.rem(record, per_shard)


def slots_of(named, per_shard):
    slots = [jnp.int32(0)] * CAP
    seen = jnp.int32(0)
    for record in range(per_shard):
        bit = (named >> record) & 1
        for slot in range(CAP):
            slots[slot] = jnp.where((bit == 1) & (seen == slot), record, slots[slot])
        seen = seen + bit
    return slots


def request_kernel(place_ref, ids_ref, enc_ref, asked_ref, *blocks, seq_count, per_shard):
    me = place_ref[0]
    core = place_ref[1] % CORES
    entries = ids_ref.shape[0] * ids_ref.shape[1] // seq_count
    width = ids_ref.shape[1]
    for distance in reversed(range(seq_count)):
        named = jnp.int32(0)
        for entry in range(entries):
            at = distance * entries + entry
            owner, local = split_record(ids_ref[at // width, at % width], per_shard)
            named = named | jnp.where(owner == me, 1 << local, 0)
        slots = slots_of(named, per_shard)
        for slot in range(CAP):
            start = pl.multiple_of(slots[slot] * RET + core * HALF, HALF)
            blocks[distance][slot] = enc_ref[pl.ds(start, HALF), :]
            if distance == 0:
                other = pl.multiple_of(slots[slot] * RET + (1 - core) * HALF, HALF)
                blocks[seq_count][slot] = enc_ref[pl.ds(other, HALF), :]
            asked_ref[distance * CAP + slot] = slots[slot]


def request(place, ids_table, encodings, seq_count):
    per_shard = encodings.shape[0] // RET
    block = jax.ShapeDtypeStruct((CAP, HALF, encodings.shape[1]), BF16)
    return pl.pallas_call(
        functools.partial(request_kernel, seq_count=seq_count, per_shard=per_shard),
        out_shape=[jax.ShapeDtypeStruct((seq_count * CAP,), jnp.int32)] + [block] * (seq_count + 1),
        in_specs=[pl.BlockSpec(memory_space=SM)] * 2 + [pl.BlockSpec(memory_space=VM)],
        out_specs=[pl.BlockSpec(memory_space=SM)]
        + [pl.BlockSpec(memory_space=VM)] * (seq_count + 1),
        compiler_params=room(encodings, *[block] * (seq_count + 1)),
        cost_estimate=pl.CostEstimate(
            flops=0, transcendentals=0, bytes_accessed=4 * encodings.size * 2
        ),
        name="request",
    )(place, ids_table, encodings)


def plan_kernel(place_ref, ids_ref, plan_ref, *, per_shard):
    me = place_ref[0]
    rows, cols = ids_ref.shape
    entries = rows * cols
    records = [ids_ref[entry // cols, entry % cols] for entry in range(entries)]
    parts = [split_record(record, per_shard) for record in records]
    bits = [1 << local for _, local in parts]
    for entry in range(entries):
        owner, local = parts[entry]
        below = jnp.int32(0)
        earlier = jnp.int32(0)
        for other in range(entries):
            below = below | jnp.where(parts[other][0] == owner, bits[other], 0)
            if other < entry:
                earlier = earlier | jnp.where(records[other] == records[entry], 1, 0)
        below = below & ((1 << local) - 1)
        rank = jnp.int32(0)
        for bit_at in range(per_shard):
            rank = rank + ((below >> bit_at) & 1)
        plan_ref[entry] = owner ^ me
        plan_ref[entries + entry] = rank
        plan_ref[2 * entries + entry] = earlier


def plan_entries(place, ids, per_shard):
    return pl.pallas_call(
        functools.partial(plan_kernel, per_shard=per_shard),
        out_shape=jax.ShapeDtypeStruct((3 * ids.size,), jnp.int32),
        in_specs=[pl.BlockSpec(memory_space=SM)] * 2,
        out_specs=pl.BlockSpec(memory_space=SM),
        compiler_params=room(),
        cost_estimate=pl.CostEstimate(flops=0, transcendentals=0, bytes_accessed=1 << 20),
        name="plan",
    )(place, ids)


def project_kernel(place_ref, *refs, count):
    pieces = refs[: 2 * count]
    wk_ref, wv_ref, key_ref, value_ref, rows, sems = refs[2 * count :]
    core = place_ref[1] % CORES

    @pl.when(pl.program_id(0) == 0)
    def _():
        copies = []
        for block in range(count):
            for source, half in ((pieces[2 * block], core), (pieces[2 * block + 1], 1 - core)):
                for slot in range(CAP):
                    at = pl.multiple_of((block * CAP + slot) * RET + half * HALF, HALF)
                    copies.append(
                        pltpu.make_async_copy(
                            source.at[slot], rows.at[pl.ds(at, HALF), :], sems.at[len(copies)]
                        )
                    )
        for copy in copies:
            copy.start()
        for copy in copies:
            copy.wait()

    for weight, target in ((wk_ref, key_ref), (wv_ref, value_ref)):
        target[...] = jnp.dot(rows[...], weight[...], preferred_element_type=F32).astype(BF16)


def project(place, pieces, w_key, w_value):
    depth, columns = w_key.shape
    count = len(pieces) // 2
    height = count * CAP * RET
    wide = min(columns, 256)
    shape = jax.ShapeDtypeStruct((height, columns), BF16)
    weight_spec = pl.BlockSpec((depth, wide), lambda i: (0, i))
    out_spec = pl.BlockSpec((height, wide), lambda i: (0, i))
    return pl.pallas_call(
        functools.partial(project_kernel, count=count),
        grid=(columns // wide,),
        out_shape=[shape, shape],
        in_specs=[pl.BlockSpec(memory_space=SM)]
        + [pl.BlockSpec(memory_space=pl.ANY)] * len(pieces)
        + [weight_spec] * 2,
        out_specs=[out_spec, out_spec],
        scratch_shapes=[
            pltpu.VMEM((height, depth), BF16),
            pltpu.SemaphoreType.DMA((len(pieces) * CAP,)),
        ],
        compiler_params=room(*pieces, shape, shape, w_key, w_value, spare=6 << 20),
        cost_estimate=pl.CostEstimate(
            flops=4 * height * w_key.size,
            transcendentals=0,
            bytes_accessed=4 * (w_key.size + height * columns),
        ),
        name="project",
    )(place, *pieces, w_key, w_value)


def attend_kernel(place_ref, plan_ref, counts_ref, q_ref, g_ref, *refs, count):
    pieces = refs[: 2 * count]
    wk_any, wv_any, key_any, value_any = refs[2 * count : 2 * count + 4]
    (
        qg_mine,
        qg_theirs,
        kv_near,
        kv_far,
        q_rows,
        g_rows,
        qg_rows,
        kv_pair,
        kv_all,
        k_ref,
        v_ref,
        enc_rows,
        wk_ref,
        wv_ref,
        sems,
    ) = refs[-15:]
    core = place_ref[1] % CORES
    rows, columns = q_ref.shape
    heads = columns // HD
    shift = SPAN - 1
    spans = rows // SPAN
    entries = spans * NEIGH
    middle = kv_near.shape[0]
    half = middle * CAP * RET
    full = rows - SPAN
    scale = 1.0 / math.sqrt(HD)
    moves = [
        (wk_any, wk_ref),
        (wv_any, wv_ref),
        (key_any.at[pl.ds(0, half), :], k_ref.at[pl.ds(0, half), :]),
        (value_any.at[pl.ds(0, half), :], v_ref.at[pl.ds(0, half), :]),
    ]
    for block in range(count):
        for source, part in ((pieces[2 * block], core), (pieces[2 * block + 1], 1 - core)):
            for slot in range(CAP):
                at = pl.multiple_of((block * CAP + slot) * RET + part * HALF, HALF)
                moves.append((source.at[slot], enc_rows.at[pl.ds(at, HALF), :]))
    copies = [
        pltpu.make_async_copy(source, target, sems.at[at])
        for at, (source, target) in enumerate(moves)
    ]
    for copy in copies:
        copy.start()
    for source, target in ((q_ref, q_rows), (g_ref, g_rows)):
        target[0:full, :] = source[shift : shift + full, :].astype(BF16)
        first = lax.broadcasted_iota(jnp.int32, (SPAN, columns), 0) == 0
        last = jnp.broadcast_to(source[rows - 1 : rows, :], (SPAN, columns))
        target[full:rows, :] = jnp.where(first, last, 0.0).astype(BF16)
    kv_all[...] = jnp.zeros_like(kv_all)
    for copy in copies:
        copy.wait()
    high = 256

    def one_block(block, carry):
        at = pl.multiple_of(block * high, high)
        enc = enc_rows[pl.ds(at, high), :]
        for weight, target in ((wk_ref, k_ref), (wv_ref, v_ref)):
            made = jnp.dot(enc, weight[...], preferred_element_type=F32).astype(BF16)
            target[pl.ds(half + at, high), :] = made
        return carry

    lax.fori_loop(0, half // high, one_block, 0)

    def one_span(span, carry):
        base = pl.multiple_of(span * SPAN, SPAN)
        two = counts_ref[span] > 1
        dist = [plan_ref[span * NEIGH + n] for n in range(NEIGH)]
        rank = [plan_ref[entries + span * NEIGH + n] for n in range(NEIGH)]
        again = [plan_ref[2 * entries + span * NEIGH + n] for n in range(NEIGH)]
        key_at = [pl.multiple_of((dist[n] * CAP + rank[n]) * RET, RET) for n in range(NEIGH)]
        column_at = lax.broadcasted_iota(jnp.int32, (SPAN, NEIGH * RET), 1)
        in_use = (column_at < RET) | two
        each = range(heads)
        lanes = [slice(head * HD, (head + 1) * HD) for head in each]
        q = [q_rows[pl.ds(base, SPAN), lanes[h]] for h in each]
        g = [g_rows[pl.ds(base, SPAN), lanes[h]] for h in each]
        k = [
            jnp.concatenate([k_ref[pl.ds(at, RET), lanes[h]] for at in key_at], axis=0)
            for h in each
        ]
        v = [
            jnp.concatenate([v_ref[pl.ds(at, RET), lanes[h]] for at in key_at], axis=0)
            for h in each
        ]
        scores = [
            lax.dot_general(q[h], k[h], NT, preferred_element_type=F32) * scale for h in each
        ]
        prob = [lax.dot_general(g[h], v[h], NT, preferred_element_type=F32) for h in each]
        scores = [jnp.where(in_use, scores[h], -jnp.inf) for h in each]
        top = [jnp.max(scores[h], axis=-1, keepdims=True) for h in each]
        exponent = [jnp.exp(scores[h] - top[h]) for h in each]
        soft = [exponent[h] / jnp.sum(exponent[h], axis=-1, keepdims=True) for h in each]
        low = [soft[h].astype(BF16) for h in each]
        out = [jnp.dot(low[h], v[h], preferred_element_type=F32) for h in each]
        vg = [lax.dot_general(g[h], low[h], TN, preferred_element_type=F32) for h in each]
        delta = [jnp.sum(g[h].astype(F32) * out[h], axis=-1, keepdims=True) for h in each]
        score_low = [(soft[h] * (prob[h] - delta[h])).astype(BF16) for h in each]
        qg = [jnp.dot(score_low[h], k[h], preferred_element_type=F32) * scale for h in each]
        kg = [
            lax.dot_general(q[h], score_low[h], TN, preferred_element_type=F32) * scale
            for h in each
        ]
        for h in each:
            qg_rows[pl.ds(base, SPAN), lanes[h]] = qg[h]
            kv_pair[lanes[h], :] = kg[h].astype(BF16)
            kv_pair[columns + h * HD : columns + (h + 1) * HD, :] = vg[h].astype(BF16)
        for n in range(NEIGH):
            made = slice(n * RET, (n + 1) * RET)
            at = pl.ds(pl.multiple_of(rank[n] * RET, RET), RET)

            @pl.when(again[n] == 0)
            def _():
                kv_all[dist[n], :, at] = kv_pair[:, made]

            @pl.when(again[n] != 0)
            def _():
                total = kv_all[dist[n], :, at].astype(F32) + kv_pair[:, made].astype(F32)
                kv_all[dist[n], :, at] = total.astype(BF16)

        return carry

    lax.fori_loop(0, spans, one_span, 0)
    copies = [
        pltpu.make_async_copy(kv_all.at[pl.ds(at * middle, middle)], target, sems.at[at])
        for at, target in enumerate((kv_near, kv_far))
    ]
    for copy in reversed(copies):
        copy.start()
    moved = jnp.concatenate(
        [jnp.zeros((shift, columns), F32), qg_rows[0 : rows - shift, :]], axis=0
    )
    qg_rows[...] = moved
    pieces, take = qg_mine.shape[:2]
    for piece in range(pieces):
        for target, which in ((qg_mine, core), (qg_theirs, 1 - core)):
            at = pl.multiple_of((piece * CORES + which) * take, take)
            target[piece] = qg_rows[pl.ds(at, take), :].astype(BF16)
    for copy in copies:
        copy.wait()


def attend(place, plan, counts, q, g, pieces, w_key, w_value, made, ready, chips):
    rows, columns = q.shape
    depth = w_key.shape[0]
    count = len(pieces) // 2
    half = made[0].shape[0]
    take = rows // (chips * CORES)
    qg = jax.ShapeDtypeStruct((chips, take, columns), BF16)
    middle = half // (CAP * RET)
    kv = jax.ShapeDtypeStruct((middle, 2 * columns, CAP * RET), BF16)
    flops = 6 * 2 * rows * NEIGH * RET * columns
    anywhere = pl.BlockSpec(memory_space=pl.ANY)
    in_hbm = pl.BlockSpec(memory_space=pltpu.MemorySpace.HBM)
    return pl.pallas_call(
        functools.partial(attend_kernel, count=count),
        out_shape=[qg, qg, kv, kv],
        in_specs=[pl.BlockSpec(memory_space=SM)] * 3
        + [pl.BlockSpec(memory_space=VM)] * 2
        + [anywhere] * (len(pieces) + 4 + len(ready)),
        out_specs=[pl.BlockSpec(memory_space=VM)] * 2 + [in_hbm] * 2,
        scratch_shapes=[
            pltpu.VMEM((rows, columns), BF16),
            pltpu.VMEM((rows, columns), BF16),
            pltpu.VMEM((rows, columns), F32),
            pltpu.VMEM((2 * columns, NEIGH * RET), BF16),
            pltpu.VMEM((2 * middle, 2 * columns, CAP * RET), BF16),
            pltpu.VMEM((2 * half, columns), BF16),
            pltpu.VMEM((2 * half, columns), BF16),
            pltpu.VMEM((half, depth), BF16),
            pltpu.VMEM((depth, columns), BF16),
            pltpu.VMEM((depth, columns), BF16),
            pltpu.SemaphoreType.DMA((4 + len(pieces) * CAP,)),
        ],
        compiler_params=room(q, g, q, q, kv, kv, *made, *made, *pieces, w_key, w_value, qg, qg, spare=8 << 20),
        cost_estimate=pl.CostEstimate(
            flops=8 * flops,
            transcendentals=rows * NEIGH * RET * columns // HD,
            bytes_accessed=8 * q.size + 8 * half * columns,
        ),
        name="attend",
    )(place, plan, counts, q, g, *pieces, w_key, w_value, *made, *ready)


def pick_kernel(place_ref, wk_ref, wv_ref, own_ref, theirs_ref):
    chips, strip, wide = own_ref.shape
    columns = wide // 2
    chip, core = place_ref[1] // CORES, place_ref[1] % CORES
    for at in range(chips):
        for target, which in ((own_ref, core), (theirs_ref, 1 - core)):
            row = pl.multiple_of(((chip ^ at) * CORES + which) * strip, strip)
            target[at, :, 0:columns] = wk_ref[pl.ds(row, strip), :]
            target[at, :, columns:wide] = wv_ref[pl.ds(row, strip), :]


def pick(place, w_key, w_value, chips):
    width, columns = w_key.shape
    strip = width // (chips * CORES)
    strips = jax.ShapeDtypeStruct((chips, strip, 2 * columns), BF16)
    return pl.pallas_call(
        pick_kernel,
        out_shape=[strips, strips],
        in_specs=[pl.BlockSpec(memory_space=SM)] + [pl.BlockSpec(memory_space=VM)] * 2,
        out_specs=[pl.BlockSpec(memory_space=VM)] * 2,
        compiler_params=room(w_key, w_value, strips, strips),
        cost_estimate=pl.CostEstimate(
            flops=0, transcendentals=0, bytes_accessed=8 * w_key.size
        ),
        name="pick",
    )(place, w_key, w_value)


def strip_parts(own_ref, other_ref, kv_ref, kv_other_ref, step, at):
    made = jnp.dot(own_ref[step], kv_ref[at], preferred_element_type=F32)
    made += jnp.dot(other_ref[step], kv_other_ref[at], preferred_element_type=F32)
    return [made[:, slot * RET : (slot + 1) * RET] for slot in range(CAP)]


def store_coded(target, base, parts):
    strip = parts[0].shape[0]
    row_at = lax.broadcasted_iota(jnp.int32, (TILE, RET), 0)
    powers = jnp.zeros((TILE, RET), jnp.int32)
    for slot, part in enumerate(parts):
        code, power = encode(part, 0)
        target[base + slot * strip : base + (slot + 1) * strip, :] = code
        powers = jnp.where(row_at == slot, power, powers)
    target[base + CAP * strip : base + CAP * strip + TILE, :] = powers.astype(I16)


def load_coded(source, base, strip):
    powers = source[base + CAP * strip : base + CAP * strip + TILE, :].astype(jnp.int32)
    return [
        decode(source[base + slot * strip : base + (slot + 1) * strip, :], powers[slot : slot + 1])
        for slot in range(CAP)
    ]


def strip_kernel(own_ref, other_ref, kv_ref, kv_other_ref, out_ref, *, step):
    height = CAP * own_ref.shape[1] + TILE
    for at in range(kv_ref.shape[0]):
        parts = strip_parts(own_ref, other_ref, kv_ref, kv_other_ref, step, at)
        store_coded(out_ref, at * height, parts)


def merge_kernel(*refs, arrived, plain):
    own_ref, other_ref, kv_ref, kv_other_ref = refs[:4]
    pieces = refs[4 : 4 + arrived]
    outs = refs[4 + arrived :]
    strip = own_ref.shape[1]
    height = CAP * strip + TILE
    for at, out_ref in enumerate(outs):
        parts = strip_parts(own_ref, other_ref, kv_ref, kv_other_ref, 0, at)
        for piece in pieces:
            more = load_coded(piece, at * height, strip)
            parts = [part + extra for part, extra in zip(parts, more)]
        if plain and at == 0:
            for slot, part in enumerate(parts):
                out_ref[slot * strip : (slot + 1) * strip, :] = part
        else:
            store_coded(out_ref, 0, parts)


def strip_of(own, other, step, kv, kv_other, arrived=(), plain=False):
    _, strip, depth = own.shape
    count = kv.shape[0]
    height = CAP * strip + TILE
    if step:
        kernel = functools.partial(strip_kernel, step=step)
        outs = [jax.ShapeDtypeStruct((count * height, RET), I16)]
    else:
        kernel = functools.partial(merge_kernel, arrived=len(arrived), plain=plain)
        outs = [jax.ShapeDtypeStruct((height, RET), I16)] * count
        if plain:
            outs[0] = jax.ShapeDtypeStruct((CAP * strip, RET), F32)
    return pl.pallas_call(
        kernel,
        out_shape=outs,
        in_specs=[pl.BlockSpec(memory_space=VM)] * (4 + len(arrived)),
        out_specs=[pl.BlockSpec(memory_space=VM)] * len(outs),
        compiler_params=room(own, other, kv, kv_other, *arrived, *outs, spare=3 << 20),
        cost_estimate=pl.CostEstimate(
            flops=4 * strip * kv.size,
            transcendentals=0,
            bytes_accessed=4 * (kv.size + strip * depth) + 4 * strip * count * CAP * RET,
        ),
        name="strip",
    )(own, other, kv, kv_other, *arrived)


def hidden_kernel(place_ref, mine_ref, theirs_ref, own_ref, near_ref, *refs):
    sends, keep_ref, total = refs[:-2], refs[-2], refs[-1]
    step = pl.program_id(0)
    take, wide = keep_ref.shape
    block = own_ref.shape[0]
    summed = jnp.zeros((total.shape[0], block), F32)
    for rows_ref, weight_ref in ((mine_ref, own_ref), (theirs_ref, near_ref)):
        part = lax.dot_general(rows_ref[...], weight_ref[...], NT, preferred_element_type=F32)
        summed = summed + part.astype(BF16).astype(F32)
    total[:, pl.ds(pl.multiple_of(step * block, block), block)] = summed

    @pl.when(step == pl.num_programs(0) - 1)
    def _():
        chip = place_ref[1] // CORES
        for at, send_ref in enumerate(sends, 1):
            row = pl.multiple_of((chip ^ at) * take, take)
            code, power = encode(total[pl.ds(row, take), :], 1)
            send_ref[:, 0:wide] = code
            send_ref[:, wide : wide + HD] = jnp.broadcast_to(power, (take, HD)).astype(I16)
        keep_ref[...] = total[pl.ds(pl.multiple_of(chip * take, take), take), :]


def hidden_rows(place, mine, theirs, w_own, w_near):
    chips, take, columns = mine.shape
    wide = w_own.shape[0]
    block = min(wide, 512)
    send = jax.ShapeDtypeStruct((take, wide + HD), I16)
    keep = jax.ShapeDtypeStruct((take, wide), F32)
    flat = [v.reshape(chips * take, columns) for v in (mine, theirs)]
    rows_spec = pl.BlockSpec(flat[0].shape, lambda i: (0, 0))
    weight_spec = pl.BlockSpec((block, columns), lambda i: (i, 0))
    total = jax.ShapeDtypeStruct((chips * take, wide), F32)
    return pl.pallas_call(
        hidden_kernel,
        grid=(wide // block,),
        out_shape=[send] * (chips - 1) + [keep],
        in_specs=[pl.BlockSpec(memory_space=SM)] + [rows_spec] * 2 + [weight_spec] * 2,
        out_specs=[pl.BlockSpec(send.shape, lambda i: (0, 0))] * (chips - 1)
        + [pl.BlockSpec(keep.shape, lambda i: (0, 0))],
        scratch_shapes=[pltpu.VMEM(total.shape, F32)],
        compiler_params=room(total, keep, keep, *[send] * (2 * chips), spare=8 << 20),
        cost_estimate=pl.CostEstimate(
            flops=4 * chips * take * w_own.size,
            transcendentals=0,
            bytes_accessed=4 * w_own.size + 8 * take * wide,
        ),
        name="hidden_rows",
    )(place, *flat, w_own, w_near)


def finish_kernel(keep_ref, *refs):
    out_ref = refs[-1]
    wide = keep_ref.shape[1]
    total = keep_ref[...]
    for piece in refs[:-1]:
        total = total + decode(piece[:, 0:wide], piece[:, wide : wide + HD][:, 0:1])
    out_ref[...] = total.astype(BF16)


def finish(keep, pieces):
    return pl.pallas_call(
        finish_kernel,
        out_shape=jax.ShapeDtypeStruct(keep.shape, BF16),
        in_specs=[pl.BlockSpec(memory_space=VM)] * (1 + len(pieces)),
        out_specs=pl.BlockSpec(memory_space=VM),
        compiler_params=room(keep, *pieces, keep),
        cost_estimate=pl.CostEstimate(
            flops=2 * keep.size, transcendentals=0, bytes_accessed=8 * keep.size
        ),
        name="finish",
    )(keep, *pieces)


def collect_kernel(asked_ref, *refs):
    blocks = refs[:-2]
    out_ref, total = refs[-2:]
    height = total.shape[0]
    total[...] = jnp.zeros_like(total)
    for distance, block in enumerate(blocks):
        if distance == 0:
            parts = [block[slot * height : (slot + 1) * height, :] for slot in range(CAP)]
        else:
            parts = load_coded(block, 0, height)
        for slot in range(CAP):
            at = pl.multiple_of(asked_ref[distance * CAP + slot] * RET, RET)
            total[:, pl.ds(at, RET)] += parts[slot]
    out_ref[...] = total[...].astype(BF16)


def collect(asked, blocks, per_shard):
    height = blocks[0].shape[0] // CAP
    return pl.pallas_call(
        collect_kernel,
        out_shape=jax.ShapeDtypeStruct((height, per_shard * RET), BF16),
        in_specs=[pl.BlockSpec(memory_space=SM)]
        + [pl.BlockSpec(memory_space=VM)] * len(blocks),
        out_specs=pl.BlockSpec(memory_space=VM),
        scratch_shapes=[pltpu.VMEM((height, per_shard * RET), F32)],
        compiler_params=room(*blocks),
        cost_estimate=pl.CostEstimate(
            flops=2 * len(blocks) * blocks[0].size,
            transcendentals=0,
            bytes_accessed=4 * len(blocks) * blocks[0].size,
        ),
        name="collect",
    )(asked, *blocks)


def shards(
    hidden_states,
    out_grad,
    encodings,
    w_query,
    w_key,
    w_value,
    w_out,
    neighbour_ids,
    neighbour_counts,
):
    seq_count = lax.axis_size("seq")
    head_count = lax.axis_size("head")
    chips = head_count // CORES
    seq_at = lax.axis_index("seq")
    head_at = lax.axis_index("head")
    place = jnp.stack([seq_at, head_at]).astype(jnp.int32)
    per_shard = encodings.shape[0] // RET
    features = hidden_states.shape[1]

    far = [(hidden_states, out_grad)]
    for step in range(1, chips):
        far.append(
            (swap(hidden_states, "head", step * CORES), swap(out_grad, "head", step * CORES))
        )
    ids_table = table_by_distance(neighbour_ids.reshape(1, -1), seq_count)
    asked, *blocks = request(place, ids_table, encodings, seq_count)
    own_half = blocks.pop()
    mine = [None] * seq_count
    for distance in reversed(range(1, seq_count)):
        mine[distance] = swap(blocks[distance], "seq", distance)
    pieces = [(blocks[0], own_half)]
    for distance in range(1, seq_count):
        pieces.append((mine[distance], swap(mine[distance], "head", 1)))
    plan = plan_entries(after(place, asked), neighbour_ids, per_shard)

    w_query_near = swap(w_query, "head", 1)
    strips, strips_theirs = pick(place, w_key, w_value, chips)
    strips_other = swap(strips_theirs, "head", 1)

    middle = seq_count // 2
    flat = [piece for pair in pieces for piece in pair]
    made = project(place, flat[: 2 * middle], w_key, w_value)

    query_sum = jnp.zeros((), F32)
    grad_sum = jnp.zeros((), F32)
    for step in range(chips):
        for side in range(CORES):
            hidden_piece, grad_piece = far[step]
            if side:
                hidden_piece = swap(hidden_piece, "head", 1)
                grad_piece = swap(grad_piece, "head", 1)
            elif step == 0:
                hidden_piece, grad_piece = after((hidden_piece, grad_piece), asked)
            block_at = (head_at ^ (step * CORES + side)) * features
            query_sum = query_sum + jnp.dot(
                hidden_piece,
                lax.dynamic_slice_in_dim(w_query, block_at, features, 0),
                preferred_element_type=F32,
            )
            grad_sum = grad_sum + lax.dot_general(
                grad_piece,
                lax.dynamic_slice_in_dim(w_out, block_at, features, 1),
                NT,
                preferred_element_type=F32,
            )

    qg_mine, qg_theirs, kv_near, kv_far = attend(
        place,
        plan,
        neighbour_counts,
        query_sum,
        grad_sum,
        flat[2 * middle :],
        w_key,
        w_value,
        made,
        (w_query_near, strips_other),
        chips,
    )
    qg_other = swap(qg_theirs, "head", 1)
    far_other = swap(kv_far, "head", 1)
    near_other = swap(kv_near, "head", 1)

    halves = ((kv_far, far_other, middle), (kv_near, near_other, 0))
    arrived = {middle: [], 0: []}
    for kv, kv_other, first in halves:
        for step in range(1, chips):
            (part,) = strip_of(strips, strips_other, step, kv, kv_other)
            part = swap(part, "head", step * CORES)
            arrived[first].append(part)
    *sends, keep = hidden_rows(place, qg_mine, qg_other, w_query, w_query_near)
    hidden_parts = [swap(part, "head", step * CORES) for step, part in enumerate(sends, 1)]
    back = [None] * seq_count
    for kv, kv_other, first in halves:
        outs = strip_of(
            strips, strips_other, 0, kv, kv_other, arrived[first], plain=first == 0
        )
        for distance, part in enumerate(outs, first):
            if distance > 0:
                part = swap(part, "seq", distance)
            back[distance] = part
    enc_grad = collect(asked, back, per_shard).T
    hidden_grad = finish(keep, hidden_parts)
    return (hidden_grad, enc_grad)


def solution(mesh):
    return jax.shard_map(
        shards,
        mesh=mesh,
        in_specs=(
            P("seq", "head"),
            P("seq", "head"),
            P("seq", None),
            P(None, "head"),
            P(None, "head"),
            P(None, "head"),
            P("head", None),
            P("seq", None),
            P("seq"),
        ),
        out_specs=(P(("seq", "head"), None), P("seq", "head")),
        check_vma=False,
    )
```

```python
import functools
import math

import jax
import jax.numpy as jnp
from jax import lax
from jax.experimental import pallas as pl
from jax.experimental.pallas import tpu as pltpu
from jax.sharding import PartitionSpec as P


HD = 128
SPAN = 64
NEIGH = 2
RET = 128
CORES = 2
CAP = 2
HALF = RET // CORES


BF16 = jnp.bfloat16
F32 = jnp.float32
I16 = jnp.int16
TILE = 16
NT = (((1,), (1,)), ((), ()))
TN = (((0,), (0,)), ((), ()))
VM = pltpu.MemorySpace.VMEM
SM = pltpu.MemorySpace.SMEM


def room(*arrays, spare=2 << 20):
    total = sum(math.prod(a.shape) * jnp.dtype(a.dtype).itemsize for a in arrays)
    return pltpu.CompilerParams(vmem_limit_bytes=int(total) + spare)


def swap(value, axis, distance):
    count = lax.axis_size(axis)
    return lax.ppermute(value, axis, [(i, i ^ distance) for i in range(count)])


def after(value, *others):
    return lax.optimization_barrier((value,) + others)[0]


def table_by_distance(row, count):
    table = row
    distance = 1
    while distance < count:
        table = jnp.concatenate([table, swap(table, "seq", distance)], axis=0)
        distance *= 2
    return table


def encode(value, axis):
    most = jnp.max(jnp.abs(value), axis=axis, keepdims=True)
    power = jnp.ceil(jnp.log2(jnp.maximum(most, 1e-30)))
    scaled = value * jnp.exp2(14.0 - power)
    code = (scaled + jnp.where(scaled >= 0, 0.5, -0.5)).astype(jnp.int32)
    return code.astype(I16), power.astype(jnp.int32)


def decode(code, power):
    unit = jnp.exp2(power.astype(jnp.int32).astype(F32) - 14.0)
    return code.astype(jnp.int32).astype(F32) * unit


def split_record(record, per_shard):
    if per_shard & (per_shard - 1) == 0:
        return record >> (per_shard.bit_length() - 1), record & (per_shard - 1)
    return lax.div(record, per_shard), lax.rem(record, per_shard)


def slots_of(named, per_shard):
    slots = [jnp.int32(0)] * CAP
    seen = jnp.int32(0)
    for record in range(per_shard):
        bit = (named >> record) & 1
        for slot in range(CAP):
            slots[slot] = jnp.where((bit == 1) & (seen == slot), record, slots[slot])
        seen = seen + bit
    return slots


def request_kernel(place_ref, ids_ref, enc_ref, asked_ref, *blocks, seq_count, per_shard):
    me = place_ref[0]
    core = place_ref[1] % CORES
    entries = ids_ref.shape[0] * ids_ref.shape[1] // seq_count
    width = ids_ref.shape[1]
    for distance in reversed(range(seq_count)):
        named = jnp.int32(0)
        for entry in range(entries):
            at = distance * entries + entry
            owner, local = split_record(ids_ref[at // width, at % width], per_shard)
            named = named | jnp.where(owner == me, 1 << local, 0)
        slots = slots_of(named, per_shard)
        for slot in range(CAP):
            start = pl.multiple_of(slots[slot] * RET + core * HALF, HALF)
            blocks[distance][slot] = enc_ref[pl.ds(start, HALF), :]
            if distance == 0:
                other = pl.multiple_of(slots[slot] * RET + (1 - core) * HALF, HALF)
                blocks[seq_count][slot] = enc_ref[pl.ds(other, HALF), :]
            asked_ref[distance * CAP + slot] = slots[slot]


def request(place, ids_table, encodings, seq_count):
    per_shard = encodings.shape[0] // RET
    block = jax.ShapeDtypeStruct((CAP, HALF, encodings.shape[1]), BF16)
    return pl.pallas_call(
        functools.partial(request_kernel, seq_count=seq_count, per_shard=per_shard),
        out_shape=[jax.ShapeDtypeStruct((seq_count * CAP,), jnp.int32)] + [block] * (seq_count + 1),
        in_specs=[pl.BlockSpec(memory_space=SM)] * 2 + [pl.BlockSpec(memory_space=VM)],
        out_specs=[pl.BlockSpec(memory_space=SM)]
        + [pl.BlockSpec(memory_space=VM)] * (seq_count + 1),
        compiler_params=room(encodings, *[block] * (seq_count + 1)),
        cost_estimate=pl.CostEstimate(
            flops=0, transcendentals=0, bytes_accessed=4 * encodings.size * 2
        ),
        name="request",
    )(place, ids_table, encodings)


def plan_kernel(place_ref, ids_ref, plan_ref, *, per_shard):
    me = place_ref[0]
    rows, cols = ids_ref.shape
    entries = rows * cols
    records = [ids_ref[entry // cols, entry % cols] for entry in range(entries)]
    parts = [split_record(record, per_shard) for record in records]
    bits = [1 << local for _, local in parts]
    for entry in range(entries):
        owner, local = parts[entry]
        below = jnp.int32(0)
        earlier = jnp.int32(0)
        for other in range(entries):
            below = below | jnp.where(parts[other][0] == owner, bits[other], 0)
            if other < entry:
                earlier = earlier | jnp.where(records[other] == records[entry], 1, 0)
        below = below & ((1 << local) - 1)
        rank = jnp.int32(0)
        for bit_at in range(per_shard):
            rank = rank + ((below >> bit_at) & 1)
        plan_ref[entry] = owner ^ me
        plan_ref[entries + entry] = rank
        plan_ref[2 * entries + entry] = earlier


def plan_entries(place, ids, per_shard):
    return pl.pallas_call(
        functools.partial(plan_kernel, per_shard=per_shard),
        out_shape=jax.ShapeDtypeStruct((3 * ids.size,), jnp.int32),
        in_specs=[pl.BlockSpec(memory_space=SM)] * 2,
        out_specs=pl.BlockSpec(memory_space=SM),
        compiler_params=room(),
        cost_estimate=pl.CostEstimate(flops=0, transcendentals=0, bytes_accessed=1 << 20),
        name="plan",
    )(place, ids)


def project_kernel(place_ref, *refs, count):
    pieces = refs[: 2 * count]
    wk_ref, wv_ref, key_ref, value_ref, rows, sems = refs[2 * count :]
    core = place_ref[1] % CORES

    @pl.when(pl.program_id(0) == 0)
    def _():
        copies = []
        for block in range(count):
            for source, half in ((pieces[2 * block], core), (pieces[2 * block + 1], 1 - core)):
                for slot in range(CAP):
                    at = pl.multiple_of((block * CAP + slot) * RET + half * HALF, HALF)
                    copies.append(
                        pltpu.make_async_copy(
                            source.at[slot], rows.at[pl.ds(at, HALF), :], sems.at[len(copies)]
                        )
                    )
        for copy in copies:
            copy.start()
        for copy in copies:
            copy.wait()

    for weight, target in ((wk_ref, key_ref), (wv_ref, value_ref)):
        target[...] = jnp.dot(rows[...], weight[...], preferred_element_type=F32).astype(BF16)


def project(place, pieces, w_key, w_value):
    depth, columns = w_key.shape
    count = len(pieces) // 2
    height = count * CAP * RET
    wide = min(columns, 256)
    shape = jax.ShapeDtypeStruct((height, columns), BF16)
    weight_spec = pl.BlockSpec((depth, wide), lambda i: (0, i))
    out_spec = pl.BlockSpec((height, wide), lambda i: (0, i))
    return pl.pallas_call(
        functools.partial(project_kernel, count=count),
        grid=(columns // wide,),
        out_shape=[shape, shape],
        in_specs=[pl.BlockSpec(memory_space=SM)]
        + [pl.BlockSpec(memory_space=pl.ANY)] * len(pieces)
        + [weight_spec] * 2,
        out_specs=[out_spec, out_spec],
        scratch_shapes=[
            pltpu.VMEM((height, depth), BF16),
            pltpu.SemaphoreType.DMA((len(pieces) * CAP,)),
        ],
        compiler_params=room(*pieces, shape, shape, w_key, w_value, spare=6 << 20),
        cost_estimate=pl.CostEstimate(
            flops=4 * height * w_key.size,
            transcendentals=0,
            bytes_accessed=4 * (w_key.size + height * columns),
        ),
        name="project",
    )(place, *pieces, w_key, w_value)


def attend_kernel(place_ref, plan_ref, counts_ref, q_ref, g_ref, *refs, count):
    pieces = refs[: 2 * count]
    wk_any, wv_any, key_any, value_any = refs[2 * count : 2 * count + 4]
    (
        qg_mine,
        qg_theirs,
        kv_near,
        kv_far,
        q_rows,
        g_rows,
        qg_rows,
        kv_pair,
        kv_all,
        k_ref,
        v_ref,
        enc_rows,
        wk_ref,
        wv_ref,
        sems,
    ) = refs[-15:]
    core = place_ref[1] % CORES
    rows, columns = q_ref.shape
    heads = columns // HD
    shift = SPAN - 1
    spans = rows // SPAN
    entries = spans * NEIGH
    middle = kv_near.shape[0]
    half = middle * CAP * RET
    full = rows - SPAN
    scale = 1.0 / math.sqrt(HD)
    moves = [
        (wk_any, wk_ref),
        (wv_any, wv_ref),
        (key_any.at[pl.ds(0, half), :], k_ref.at[pl.ds(0, half), :]),
        (value_any.at[pl.ds(0, half), :], v_ref.at[pl.ds(0, half), :]),
    ]
    for block in range(count):
        for source, part in ((pieces[2 * block], core), (pieces[2 * block + 1], 1 - core)):
            for slot in range(CAP):
                at = pl.multiple_of((block * CAP + slot) * RET + part * HALF, HALF)
                moves.append((source.at[slot], enc_rows.at[pl.ds(at, HALF), :]))
    copies = [
        pltpu.make_async_copy(source, target, sems.at[at])
        for at, (source, target) in enumerate(moves)
    ]
    for copy in copies:
        copy.start()
    for source, target in ((q_ref, q_rows), (g_ref, g_rows)):
        target[0:full, :] = source[shift : shift + full, :].astype(BF16)
        first = lax.broadcasted_iota(jnp.int32, (SPAN, columns), 0) == 0
        last = jnp.broadcast_to(source[rows - 1 : rows, :], (SPAN, columns))
        target[full:rows, :] = jnp.where(first, last, 0.0).astype(BF16)
    kv_all[...] = jnp.zeros_like(kv_all)
    for copy in copies:
        copy.wait()
    high = 256

    def one_block(block, carry):
        at = pl.multiple_of(block * high, high)
        enc = enc_rows[pl.ds(at, high), :]
        for weight, target in ((wk_ref, k_ref), (wv_ref, v_ref)):
            made = jnp.dot(enc, weight[...], preferred_element_type=F32).astype(BF16)
            target[pl.ds(half + at, high), :] = made
        return carry

    lax.fori_loop(0, half // high, one_block, 0)

    def one_span(span, carry):
        base = pl.multiple_of(span * SPAN, SPAN)
        two = counts_ref[span] > 1
        dist = [plan_ref[span * NEIGH + n] for n in range(NEIGH)]
        rank = [plan_ref[entries + span * NEIGH + n] for n in range(NEIGH)]
        again = [plan_ref[2 * entries + span * NEIGH + n] for n in range(NEIGH)]
        key_at = [pl.multiple_of((dist[n] * CAP + rank[n]) * RET, RET) for n in range(NEIGH)]
        column_at = lax.broadcasted_iota(jnp.int32, (SPAN, NEIGH * RET), 1)
        in_use = (column_at < RET) | two
        each = range(heads)
        lanes = [slice(head * HD, (head + 1) * HD) for head in each]
        q = [q_rows[pl.ds(base, SPAN), lanes[h]] for h in each]
        g = [g_rows[pl.ds(base, SPAN), lanes[h]] for h in each]
        k = [
            jnp.concatenate([k_ref[pl.ds(at, RET), lanes[h]] for at in key_at], axis=0)
            for h in each
        ]
        v = [
            jnp.concatenate([v_ref[pl.ds(at, RET), lanes[h]] for at in key_at], axis=0)
            for h in each
        ]
        scores = [
            lax.dot_general(q[h], k[h], NT, preferred_element_type=F32) * scale for h in each
        ]
        prob = [lax.dot_general(g[h], v[h], NT, preferred_element_type=F32) for h in each]
        scores = [jnp.where(in_use, scores[h], -jnp.inf) for h in each]
        top = [jnp.max(scores[h], axis=-1, keepdims=True) for h in each]
        exponent = [jnp.exp(scores[h] - top[h]) for h in each]
        soft = [exponent[h] / jnp.sum(exponent[h], axis=-1, keepdims=True) for h in each]
        low = [soft[h].astype(BF16) for h in each]
        out = [jnp.dot(low[h], v[h], preferred_element_type=F32) for h in each]
        vg = [lax.dot_general(g[h], low[h], TN, preferred_element_type=F32) for h in each]
        delta = [jnp.sum(g[h].astype(F32) * out[h], axis=-1, keepdims=True) for h in each]
        score_low = [(soft[h] * (prob[h] - delta[h])).astype(BF16) for h in each]
        qg = [jnp.dot(score_low[h], k[h], preferred_element_type=F32) * scale for h in each]
        kg = [
            lax.dot_general(q[h], score_low[h], TN, preferred_element_type=F32) * scale
            for h in each
        ]
        for h in each:
            qg_rows[pl.ds(base, SPAN), lanes[h]] = qg[h]
            kv_pair[lanes[h], :] = kg[h].astype(BF16)
            kv_pair[columns + h * HD : columns + (h + 1) * HD, :] = vg[h].astype(BF16)
        for n in range(NEIGH):
            made = slice(n * RET, (n + 1) * RET)
            at = pl.ds(pl.multiple_of(rank[n] * RET, RET), RET)

            @pl.when(again[n] == 0)
            def _():
                kv_all[dist[n], :, at] = kv_pair[:, made]

            @pl.when(again[n] != 0)
            def _():
                total = kv_all[dist[n], :, at].astype(F32) + kv_pair[:, made].astype(F32)
                kv_all[dist[n], :, at] = total.astype(BF16)

        return carry

    lax.fori_loop(0, spans, one_span, 0)
    copies = [
        pltpu.make_async_copy(kv_all.at[pl.ds(at * middle, middle)], target, sems.at[at])
        for at, target in enumerate((kv_near, kv_far))
    ]
    for copy in reversed(copies):
        copy.start()
    moved = jnp.concatenate(
        [jnp.zeros((shift, columns), F32), qg_rows[0 : rows - shift, :]], axis=0
    )
    qg_rows[...] = moved
    pieces, take = qg_mine.shape[:2]
    for piece in range(pieces):
        for target, which in ((qg_mine, core), (qg_theirs, 1 - core)):
            at = pl.multiple_of((piece * CORES + which) * take, take)
            target[piece] = qg_rows[pl.ds(at, take), :].astype(BF16)
    for copy in copies:
        copy.wait()


def attend(place, plan, counts, q, g, pieces, w_key, w_value, made, ready, chips):
    rows, columns = q.shape
    depth = w_key.shape[0]
    count = len(pieces) // 2
    half = made[0].shape[0]
    take = rows // (chips * CORES)
    qg = jax.ShapeDtypeStruct((chips, take, columns), BF16)
    middle = half // (CAP * RET)
    kv = jax.ShapeDtypeStruct((middle, 2 * columns, CAP * RET), BF16)
    flops = 6 * 2 * rows * NEIGH * RET * columns
    anywhere = pl.BlockSpec(memory_space=pl.ANY)
    in_hbm = pl.BlockSpec(memory_space=pltpu.MemorySpace.HBM)
    return pl.pallas_call(
        functools.partial(attend_kernel, count=count),
        out_shape=[qg, qg, kv, kv],
        in_specs=[pl.BlockSpec(memory_space=SM)] * 3
        + [pl.BlockSpec(memory_space=VM)] * 2
        + [anywhere] * (len(pieces) + 4 + len(ready)),
        out_specs=[pl.BlockSpec(memory_space=VM)] * 2 + [in_hbm] * 2,
        scratch_shapes=[
            pltpu.VMEM((rows, columns), BF16),
            pltpu.VMEM((rows, columns), BF16),
            pltpu.VMEM((rows, columns), F32),
            pltpu.VMEM((2 * columns, NEIGH * RET), BF16),
            pltpu.VMEM((2 * middle, 2 * columns, CAP * RET), BF16),
            pltpu.VMEM((2 * half, columns), BF16),
            pltpu.VMEM((2 * half, columns), BF16),
            pltpu.VMEM((half, depth), BF16),
            pltpu.VMEM((depth, columns), BF16),
            pltpu.VMEM((depth, columns), BF16),
            pltpu.SemaphoreType.DMA((4 + len(pieces) * CAP,)),
        ],
        compiler_params=room(q, g, q, q, kv, kv, *made, *made, *pieces, w_key, w_value, qg, qg, spare=8 << 20),
        cost_estimate=pl.CostEstimate(
            flops=8 * flops,
            transcendentals=rows * NEIGH * RET * columns // HD,
            bytes_accessed=8 * q.size + 8 * half * columns,
        ),
        name="attend",
    )(place, plan, counts, q, g, *pieces, w_key, w_value, *made, *ready)


def pick_kernel(place_ref, wk_ref, wv_ref, own_ref, theirs_ref):
    chips, strip, wide = own_ref.shape
    columns = wide // 2
    chip, core = place_ref[1] // CORES, place_ref[1] % CORES
    for at in range(chips):
        for target, which in ((own_ref, core), (theirs_ref, 1 - core)):
            row = pl.multiple_of(((chip ^ at) * CORES + which) * strip, strip)
            target[at, :, 0:columns] = wk_ref[pl.ds(row, strip), :]
            target[at, :, columns:wide] = wv_ref[pl.ds(row, strip), :]


def pick(place, w_key, w_value, chips):
    width, columns = w_key.shape
    strip = width // (chips * CORES)
    strips = jax.ShapeDtypeStruct((chips, strip, 2 * columns), BF16)
    return pl.pallas_call(
        pick_kernel,
        out_shape=[strips, strips],
        in_specs=[pl.BlockSpec(memory_space=SM)] + [pl.BlockSpec(memory_space=VM)] * 2,
        out_specs=[pl.BlockSpec(memory_space=VM)] * 2,
        compiler_params=room(w_key, w_value, strips, strips),
        cost_estimate=pl.CostEstimate(
            flops=0, transcendentals=0, bytes_accessed=8 * w_key.size
        ),
        name="pick",
    )(place, w_key, w_value)


def strip_parts(own_ref, other_ref, kv_ref, kv_other_ref, step, at):
    made = jnp.dot(own_ref[step], kv_ref[at], preferred_element_type=F32)
    made += jnp.dot(other_ref[step], kv_other_ref[at], preferred_element_type=F32)
    return [made[:, slot * RET : (slot + 1) * RET] for slot in range(CAP)]


def store_coded(target, base, parts):
    strip = parts[0].shape[0]
    row_at = lax.broadcasted_iota(jnp.int32, (TILE, RET), 0)
    powers = jnp.zeros((TILE, RET), jnp.int32)
    for slot, part in enumerate(parts):
        code, power = encode(part, 0)
        target[base + slot * strip : base + (slot + 1) * strip, :] = code
        powers = jnp.where(row_at == slot, power, powers)
    target[base + CAP * strip : base + CAP * strip + TILE, :] = powers.astype(I16)


def load_coded(source, base, strip):
    powers = source[base + CAP * strip : base + CAP * strip + TILE, :].astype(jnp.int32)
    return [
        decode(source[base + slot * strip : base + (slot + 1) * strip, :], powers[slot : slot + 1])
        for slot in range(CAP)
    ]


def strip_kernel(own_ref, other_ref, kv_ref, kv_other_ref, out_ref, *, step):
    height = CAP * own_ref.shape[1] + TILE
    for at in range(kv_ref.shape[0]):
        parts = strip_parts(own_ref, other_ref, kv_ref, kv_other_ref, step, at)
        store_coded(out_ref, at * height, parts)


def merge_kernel(*refs, arrived, plain):
    own_ref, other_ref, kv_ref, kv_other_ref = refs[:4]
    pieces = refs[4 : 4 + arrived]
    outs = refs[4 + arrived :]
    strip = own_ref.shape[1]
    height = CAP * strip + TILE
    for at, out_ref in enumerate(outs):
        parts = strip_parts(own_ref, other_ref, kv_ref, kv_other_ref, 0, at)
        for piece in pieces:
            more = load_coded(piece, at * height, strip)
            parts = [part + extra for part, extra in zip(parts, more)]
        if plain and at == 0:
            for slot, part in enumerate(parts):
                out_ref[slot * strip : (slot + 1) * strip, :] = part
        else:
            store_coded(out_ref, 0, parts)


def strip_of(own, other, step, kv, kv_other, arrived=(), plain=False):
    _, strip, depth = own.shape
    count = kv.shape[0]
    height = CAP * strip + TILE
    if step:
        kernel = functools.partial(strip_kernel, step=step)
        outs = [jax.ShapeDtypeStruct((count * height, RET), I16)]
    else:
        kernel = functools.partial(merge_kernel, arrived=len(arrived), plain=plain)
        outs = [jax.ShapeDtypeStruct((height, RET), I16)] * count
        if plain:
            outs[0] = jax.ShapeDtypeStruct((CAP * strip, RET), F32)
    return pl.pallas_call(
        kernel,
        out_shape=outs,
        in_specs=[pl.BlockSpec(memory_space=VM)] * (4 + len(arrived)),
        out_specs=[pl.BlockSpec(memory_space=VM)] * len(outs),
        compiler_params=room(own, other, kv, kv_other, *arrived, *outs, spare=3 << 20),
        cost_estimate=pl.CostEstimate(
            flops=4 * strip * kv.size,
            transcendentals=0,
            bytes_accessed=4 * (kv.size + strip * depth) + 4 * strip * count * CAP * RET,
        ),
        name="strip",
    )(own, other, kv, kv_other, *arrived)


def near_kernel(own_ref, other_ref, kv_ref, kv_other_ref, *outs):
    chips, strip, _ = own_ref.shape
    height = CAP * strip + TILE
    for at, out_ref in enumerate(outs):
        for step in range(chips):
            parts = strip_parts(own_ref, other_ref, kv_ref, kv_other_ref, step, at)
            if at == 0:
                for slot, part in enumerate(parts):
                    row = (step * CAP + slot) * strip
                    out_ref[row : row + strip, :] = part
            else:
                store_coded(out_ref, step * height, parts)


def near_strips(own, other, kv, kv_other):
    chips, strip, depth = own.shape
    count = kv.shape[0]
    outs = [jax.ShapeDtypeStruct((chips * CAP * strip, RET), F32)]
    outs += [jax.ShapeDtypeStruct((chips * (CAP * strip + TILE), RET), I16)] * (count - 1)
    return pl.pallas_call(
        near_kernel,
        out_shape=outs,
        in_specs=[pl.BlockSpec(memory_space=VM)] * 4,
        out_specs=[pl.BlockSpec(memory_space=VM)] * len(outs),
        compiler_params=room(own, other, kv, kv_other, *outs, spare=3 << 20),
        cost_estimate=pl.CostEstimate(
            flops=4 * chips * strip * kv.size,
            transcendentals=0,
            bytes_accessed=4 * (kv.size + chips * strip * depth),
        ),
        name="near",
    )(own, other, kv, kv_other)


def gather_kernel(asked_ref, *refs, chips):
    blocks, keep_ref, sends, total = refs[: -chips - 1], refs[-chips - 1], refs[-chips:-1], refs[-1]
    strip = keep_ref.shape[0]
    height = CAP * strip + TILE
    for step in range(chips):
        total[...] = jnp.zeros_like(total)
        for distance, block in enumerate(blocks):
            if distance == 0:
                rows = [(step * CAP + slot) * strip for slot in range(CAP)]
                parts = [block[row : row + strip, :] for row in rows]
            else:
                parts = load_coded(block, step * height, strip)
            for slot in range(CAP):
                at = pl.multiple_of(asked_ref[distance * CAP + slot] * RET, RET)
                total[:, pl.ds(at, RET)] += parts[slot]
        if step == 0:
            keep_ref[...] = total[...]
        else:
            code, power = encode(total[...], 0)
            sends[step - 1][0:strip, :] = code
            sends[step - 1][strip : strip + TILE, :] = jnp.broadcast_to(
                power, (TILE, power.shape[1])
            ).astype(I16)


def gather(asked, blocks, chips, per_shard):
    strip = blocks[0].shape[0] // (chips * CAP)
    wide = per_shard * RET
    keep = jax.ShapeDtypeStruct((strip, wide), F32)
    send = jax.ShapeDtypeStruct((strip + TILE, wide), I16)
    return pl.pallas_call(
        functools.partial(gather_kernel, chips=chips),
        out_shape=[keep] + [send] * (chips - 1),
        in_specs=[pl.BlockSpec(memory_space=SM)] + [pl.BlockSpec(memory_space=VM)] * len(blocks),
        out_specs=[pl.BlockSpec(memory_space=VM)] * chips,
        scratch_shapes=[pltpu.VMEM((strip, wide), F32)],
        compiler_params=room(*blocks, keep, keep, *[send] * (chips - 1)),
        cost_estimate=pl.CostEstimate(
            flops=4 * len(blocks) * blocks[0].size,
            transcendentals=0,
            bytes_accessed=4 * len(blocks) * blocks[0].size,
        ),
        name="gather",
    )(asked, *blocks)


def hidden_kernel(place_ref, mine_ref, theirs_ref, own_ref, near_ref, *refs):
    sends, keep_ref, total = refs[:-2], refs[-2], refs[-1]
    step = pl.program_id(0)
    take, wide = keep_ref.shape
    block = own_ref.shape[0]
    summed = jnp.zeros((total.shape[0], block), F32)
    for rows_ref, weight_ref in ((mine_ref, own_ref), (theirs_ref, near_ref)):
        part = lax.dot_general(rows_ref[...], weight_ref[...], NT, preferred_element_type=F32)
        summed = summed + part.astype(BF16).astype(F32)
    total[:, pl.ds(pl.multiple_of(step * block, block), block)] = summed

    @pl.when(step == pl.num_programs(0) - 1)
    def _():
        chip = place_ref[1] // CORES
        for at, send_ref in enumerate(sends, 1):
            row = pl.multiple_of((chip ^ at) * take, take)
            code, power = encode(total[pl.ds(row, take), :], 1)
            send_ref[:, 0:wide] = code
            send_ref[:, wide : wide + HD] = jnp.broadcast_to(power, (take, HD)).astype(I16)
        keep_ref[...] = total[pl.ds(pl.multiple_of(chip * take, take), take), :]


def hidden_rows(place, mine, theirs, w_own, w_near):
    chips, take, columns = mine.shape
    wide = w_own.shape[0]
    block = min(wide, 1024)
    send = jax.ShapeDtypeStruct((take, wide + HD), I16)
    keep = jax.ShapeDtypeStruct((take, wide), F32)
    flat = [v.reshape(chips * take, columns) for v in (mine, theirs)]
    rows_spec = pl.BlockSpec(flat[0].shape, lambda i: (0, 0))
    weight_spec = pl.BlockSpec((block, columns), lambda i: (i, 0))
    total = jax.ShapeDtypeStruct((chips * take, wide), F32)
    return pl.pallas_call(
        hidden_kernel,
        grid=(wide // block,),
        out_shape=[send] * (chips - 1) + [keep],
        in_specs=[pl.BlockSpec(memory_space=SM)] + [rows_spec] * 2 + [weight_spec] * 2,
        out_specs=[pl.BlockSpec(send.shape, lambda i: (0, 0))] * (chips - 1)
        + [pl.BlockSpec(keep.shape, lambda i: (0, 0))],
        scratch_shapes=[pltpu.VMEM(total.shape, F32)],
        compiler_params=room(total, keep, keep, *[send] * (2 * chips), spare=8 << 20),
        cost_estimate=pl.CostEstimate(
            flops=4 * chips * take * w_own.size,
            transcendentals=0,
            bytes_accessed=4 * w_own.size + 8 * take * wide,
        ),
        name="hidden_rows",
    )(place, *flat, w_own, w_near)


def finish_kernel(keep_ref, *refs):
    out_ref = refs[-1]
    wide = keep_ref.shape[1]
    total = keep_ref[...]
    for piece in refs[:-1]:
        total = total + decode(piece[:, 0:wide], piece[:, wide : wide + HD][:, 0:1])
    out_ref[...] = total.astype(BF16)


def finish(keep, pieces):
    return pl.pallas_call(
        finish_kernel,
        out_shape=jax.ShapeDtypeStruct(keep.shape, BF16),
        in_specs=[pl.BlockSpec(memory_space=VM)] * (1 + len(pieces)),
        out_specs=pl.BlockSpec(memory_space=VM),
        compiler_params=room(keep, *pieces, keep),
        cost_estimate=pl.CostEstimate(
            flops=2 * keep.size, transcendentals=0, bytes_accessed=8 * keep.size
        ),
        name="finish",
    )(keep, *pieces)


def collect_kernel(asked_ref, keep_ref, *refs, first):
    out_ref, total = refs[-2:]
    strip = keep_ref.shape[0]
    count = len(refs) - 2
    total[...] = keep_ref[...]
    for distance, block in enumerate(refs[:count]):
        if block.shape[1] == total.shape[1]:
            power = block[strip : strip + TILE, :].astype(jnp.int32)[0:1]
            total[...] += decode(block[0:strip, :], power)
            continue
        parts = load_coded(block, 0, strip)
        for slot in range(CAP):
            at = pl.multiple_of(asked_ref[(first + distance) * CAP + slot] * RET, RET)
            total[:, pl.ds(at, RET)] += parts[slot]
    out_ref[...] = total[...].astype(BF16)


def collect(asked, keep, far, sums, first):
    blocks = list(far) + list(sums)
    return pl.pallas_call(
        functools.partial(collect_kernel, first=first),
        out_shape=jax.ShapeDtypeStruct(keep.shape, BF16),
        in_specs=[pl.BlockSpec(memory_space=SM)]
        + [pl.BlockSpec(memory_space=VM)] * (1 + len(blocks)),
        out_specs=pl.BlockSpec(memory_space=VM),
        scratch_shapes=[pltpu.VMEM(keep.shape, F32)],
        compiler_params=room(keep, keep, *blocks),
        cost_estimate=pl.CostEstimate(
            flops=2 * len(blocks) * blocks[0].size,
            transcendentals=0,
            bytes_accessed=4 * len(blocks) * blocks[0].size,
        ),
        name="collect",
    )(asked, keep, *blocks)


def shards(
    hidden_states,
    out_grad,
    encodings,
    w_query,
    w_key,
    w_value,
    w_out,
    neighbour_ids,
    neighbour_counts,
):
    seq_count = lax.axis_size("seq")
    head_count = lax.axis_size("head")
    chips = head_count // CORES
    seq_at = lax.axis_index("seq")
    head_at = lax.axis_index("head")
    place = jnp.stack([seq_at, head_at]).astype(jnp.int32)
    per_shard = encodings.shape[0] // RET
    features = hidden_states.shape[1]

    far = [(hidden_states, out_grad)]
    for step in range(1, chips):
        far.append(
            (swap(hidden_states, "head", step * CORES), swap(out_grad, "head", step * CORES))
        )
    ids_table = table_by_distance(neighbour_ids.reshape(1, -1), seq_count)
    asked, *blocks = request(place, ids_table, encodings, seq_count)
    own_half = blocks.pop()
    mine = [None] * seq_count
    for distance in reversed(range(1, seq_count)):
        mine[distance] = swap(blocks[distance], "seq", distance)
    pieces = [(blocks[0], own_half)]
    for distance in range(1, seq_count):
        pieces.append((mine[distance], swap(mine[distance], "head", 1)))
    plan = plan_entries(after(place, asked), neighbour_ids, per_shard)

    w_query_near = swap(w_query, "head", 1)
    strips, strips_theirs = pick(place, w_key, w_value, chips)
    strips_other = swap(strips_theirs, "head", 1)

    middle = seq_count // 2
    flat = [piece for pair in pieces for piece in pair]
    made = project(place, flat[: 2 * middle], w_key, w_value)

    query_sum = jnp.zeros((), F32)
    grad_sum = jnp.zeros((), F32)
    for step in range(chips):
        for side in range(CORES):
            hidden_piece, grad_piece = far[step]
            if side:
                hidden_piece = swap(hidden_piece, "head", 1)
                grad_piece = swap(grad_piece, "head", 1)
            elif step == 0:
                hidden_piece, grad_piece = after((hidden_piece, grad_piece), asked)
            block_at = (head_at ^ (step * CORES + side)) * features
            query_sum = query_sum + jnp.dot(
                hidden_piece,
                lax.dynamic_slice_in_dim(w_query, block_at, features, 0),
                preferred_element_type=F32,
            )
            grad_sum = grad_sum + lax.dot_general(
                grad_piece,
                lax.dynamic_slice_in_dim(w_out, block_at, features, 1),
                NT,
                preferred_element_type=F32,
            )

    qg_mine, qg_theirs, kv_near, kv_far = attend(
        place,
        plan,
        neighbour_counts,
        query_sum,
        grad_sum,
        flat[2 * middle :],
        w_key,
        w_value,
        made,
        (w_query_near, strips_other),
        chips,
    )
    qg_other = swap(qg_theirs, "head", 1)
    far_other = swap(kv_far, "head", 1)
    near_other = swap(kv_near, "head", 1)

    arrived = []
    for step in range(1, chips):
        (part,) = strip_of(strips, strips_other, step, kv_far, far_other)
        arrived.append(swap(part, "head", step * CORES))
    near = near_strips(strips, strips_other, kv_near, near_other)
    near = [near[0]] + [swap(near[distance], "seq", distance) for distance in range(1, middle)]
    *sends, keep = hidden_rows(place, qg_mine, qg_other, w_query, w_query_near)
    hidden_parts = [swap(part, "head", step * CORES) for step, part in enumerate(sends, 1)]
    far = strip_of(strips, strips_other, 0, kv_far, far_other, arrived)
    far = [swap(part, "seq", distance) for distance, part in enumerate(far, middle)]
    per_shard = encodings.shape[0] // RET
    enc_keep, *sums = gather(asked, near, chips, per_shard)
    sums = [swap(part, "head", step * CORES) for step, part in enumerate(sums, 1)]
    enc_grad = collect(asked, enc_keep, far, sums, middle).T
    hidden_grad = finish(keep, hidden_parts)
    return (hidden_grad, enc_grad)


def solution(mesh):
    return jax.shard_map(
        shards,
        mesh=mesh,
        in_specs=(
            P("seq", "head"),
            P("seq", "head"),
            P("seq", None),
            P(None, "head"),
            P(None, "head"),
            P(None, "head"),
            P("head", None),
            P("seq", None),
            P("seq"),
        ),
        out_specs=(P(("seq", "head"), None), P("seq", "head")),
        check_vma=False,
    )
```
